256 devices in a mesh: ty: 8 (over y, core), tx: 32 (over z, x).
Axes of the slice: x: 4, y: 4, z: 8, core: 2. Of those that a mesh axis runs over, the one named last changes fastest.
Arguments:
- object_field: float32 [2, 2, 3072, 12288], P(None, None, 'ty', 'tx'), may hold values from -5 to 5
- probe_wave: float32 [2, 256, 256], replicated, may hold values from -6 to 6
- prop_phase: float32 [256, 256], replicated, may hold values from -3.140625 to 3.140625
- amplitude: float32 [1024, 256, 256], P(('ty', 'tx')), may hold values from 0.1 to 3
- offsets: int32 [2, 1024], P(None, ('ty', 'tx')), may hold values from 0 to 383, as said below
- live_slots: int32 [1024], P(('ty', 'tx')), may hold values from 0 to 1, as said below
Outputs:
- object_grad: float32 [2, 2, 3072, 12288], P(None, None, 'ty', 'tx')
- probe_grad: float32 [2, 256, 256], replicated
The draws below stay inside these ranges and needn't reach their ends.
Inputs may be any that keep to these rules, and one draw needn't show every extreme that they name: `offsets`: offsets of row and column of a window inside its device's tile; on devices of the last row of ty the row offset is at most 128, on the last column of tx the column offset likewise, so every window lies inside the object. `live_slots`: each device has between 1 and 4 live slots, in any of its slots; some device has exactly 4.
All inputs are finite; a program needn't handle non-finite values.
Results may differ from the reference program's by a relative error of at most 0.0003.
Values sent between devices are 32-bit elements; how exact they have to be, the bound alone decides.
A program may use at most 128 MiB of HBM per device.

```python
import math
import jax
import jax.numpy as jnp
from jax import lax

PATCH = 256
SLICES = 2
TILE = 384
MAXPOS = 4
OY = 3072
OX = 12288
SLOTS = 1024
N_TY = 8
N_TX = 32


def draw_offsets(key, part):
    slots = MAXPOS * N_TY * N_TX
    keys = jax.random.split(jax.random.fold_in(key, 11), 4)
    slot_ids = jnp.arange(slots, dtype=jnp.int32)
    device = slot_ids // MAXPOS
    row_ids = device // N_TX
    col_ids = device % N_TX
    inner = jax.random.randint(keys[0], (2, slots), 0, TILE, dtype=jnp.int32)
    edged = jax.random.randint(keys[1], (2, slots), 0, TILE - PATCH + 1, dtype=jnp.int32)
    at_edge = jnp.stack([row_ids == N_TY - 1, col_ids == N_TX - 1])
    chosen = jnp.where(at_edge, edged, inner)
    pick_row = jax.random.randint(keys[2], (), 0, N_TY - 1, dtype=jnp.int32)
    pick_col = jax.random.randint(keys[3], (), 0, N_TX - 1, dtype=jnp.int32)
    target = (pick_row * N_TX + pick_col) * MAXPOS
    chosen = chosen.at[:, target].set(TILE - 1)
    chosen = chosen.at[:, target + 1].set(0)
    return chosen.astype(jnp.int32)


def draw_live_slots(key, part):
    devices = N_TY * N_TX
    keys = jax.random.split(jax.random.fold_in(key, 23), 3)
    counts = jax.random.randint(keys[0], (devices,), 1, MAXPOS + 1, dtype=jnp.int32)
    busiest = jax.random.randint(keys[1], (), 0, devices, dtype=jnp.int32)
    counts = counts.at[busiest].set(MAXPOS)
    scores = jax.random.randint(keys[2], (devices, MAXPOS), 0, 1 << 20, dtype=jnp.int32) * MAXPOS
    scores = scores + jnp.arange(MAXPOS, dtype=jnp.int32)[None, :]
    ranks = jnp.argsort(jnp.argsort(scores, axis=1), axis=1)
    return (ranks < counts[:, None]).astype(jnp.int32).reshape(-1)


def block_scale(key, shape, cuts, smallest, largest):
    gain = 1.0
    for position, blocks in cuts:
        steps = jax.random.uniform(jax.random.fold_in(jax.random.fold_in(key, 6), position), (blocks,), jnp.float32, smallest / len(cuts), largest / len(cuts))
        gain = gain * jnp.repeat(jnp.exp(steps), shape[position] // blocks).reshape((-1,) + (1,) * (len(shape) - 1 - position))
    return gain


def gaussian(rng, extent, scale, bound, cuts=(), kind=jnp.bfloat16):
    values = jax.random.normal(rng, extent, jnp.float32) * scale
    if len(cuts) > 0:
        values = block_scale(rng, extent, cuts, -0.22, 0.18) * values
    return jnp.clip(values, min=-bound, max=bound).astype(kind)


def setup_inputs(seed: int = 0) -> dict:
    key_of = jax.random.split(jax.random.key(seed), 7)
    return {
        "object_field": gaussian(key_of[0], (SLICES, 2, OY, OX), 0.7, 5.0, ((2, 8), (3, 32)), jnp.float32),
        "probe_wave": gaussian(key_of[1], (2, PATCH, PATCH), 1.0, 6.0, (), jnp.float32),
        "prop_phase": jnp.clip(jax.random.uniform(key_of[2], (PATCH, PATCH), jnp.float32, -3.140625, 3.140625), -3.140625, 3.140625),
        "amplitude": jnp.clip(jnp.exp(math.log(3.0) - 3.4011974 * jax.random.uniform(key_of[3], (SLOTS, PATCH, PATCH), jnp.float32) ** block_scale(key_of[3], (SLOTS, PATCH, PATCH), ((0, 256),), -0.2, 0.2)), 0.1, 3.0),
        "offsets": draw_offsets(jax.random.fold_in(key_of[6], 71), 0),
        "live_slots": draw_live_slots(jax.random.fold_in(key_of[6], 71), 0),
    }


def dft_tables(length):
    indices = jnp.arange(length, dtype=jnp.int32)
    product = indices[:, None] * indices[None, :] % length
    angles = product.astype(jnp.float32) * (2.0 * math.pi / length)
    factor = 1.0 / math.sqrt(length)
    return (jnp.cos(angles) * factor, jnp.sin(angles) * factor)

def matmul(left, right):
    return jnp.dot(left, right, precision=lax.Precision.HIGHEST, preferred_element_type=jnp.float32)

def transform(real_part, imag_part, cosine, sine_table, orient):
    half_real = matmul(real_part, cosine) - orient * matmul(imag_part, sine_table)
    half_imag = matmul(imag_part, cosine) + orient * matmul(real_part, sine_table)
    full_real = matmul(cosine, half_real) - orient * matmul(sine_table, half_imag)
    full_imag = matmul(cosine, half_imag) + orient * matmul(sine_table, half_real)
    return (full_real, full_imag)

def patch_gradient(window, probe_wave, prop_real, prop_imag, measured, cosine, sine_table):
    layers = window.shape[0]
    wave_real, wave_imag = (probe_wave[0], probe_wave[1])
    incident = []
    for layer_index in range(layers):
        trans_real, trans_imag = (window[layer_index, 0], window[layer_index, 1])
        incident.append((wave_real, wave_imag))
        exit_real = trans_real * wave_real - trans_imag * wave_imag
        exit_imag = trans_real * wave_imag + trans_imag * wave_real
        freq_real, freq_imag = transform(exit_real, exit_imag, cosine, sine_table, -1.0)
        if layer_index + 1 < layers:
            kept_real = prop_real * freq_real - prop_imag * freq_imag
            kept_imag = prop_real * freq_imag + prop_imag * freq_real
            wave_real, wave_imag = transform(kept_real, kept_imag, cosine, sine_table, 1.0)
    modulus = jnp.sqrt(freq_real * freq_real + freq_imag * freq_imag + 0.25)
    factor = measured / modulus - 1.0
    back_real, back_imag = transform(freq_real * factor, freq_imag * factor, cosine, sine_table, 1.0)
    pieces = [None] * layers
    probe_real, probe_imag = (back_real, back_imag)
    for layer_index in reversed(range(layers)):
        inc_real, inc_imag = incident[layer_index]
        trans_real, trans_imag = (window[layer_index, 0], window[layer_index, 1])
        pieces[layer_index] = jnp.stack([inc_real * back_real + inc_imag * back_imag, inc_real * back_imag - inc_imag * back_real])
        delta_real = trans_real * back_real + trans_imag * back_imag
        delta_imag = trans_real * back_imag - trans_imag * back_real
        if layer_index > 0:
            upper_real, upper_imag = transform(delta_real, delta_imag, cosine, sine_table, -1.0)
            moved_real = prop_real * upper_real + prop_imag * upper_imag
            moved_imag = prop_real * upper_imag - prop_imag * upper_real
            back_real, back_imag = transform(moved_real, moved_imag, cosine, sine_table, 1.0)
        else:
            probe_real, probe_imag = (delta_real, delta_imag)
    return (jnp.stack(pieces), jnp.stack([probe_real, probe_imag]))

def reference(object_field, probe_wave, prop_phase, amplitude, offsets, live_slots):
    cosine, sine_table = dft_tables(PATCH)
    prop_real = jnp.cos(prop_phase)
    prop_imag = jnp.sin(prop_phase)
    anchor = jnp.zeros((), jnp.int32)

    def visit(carry, slot_index):
        gradient, probe_total = carry
        device = slot_index // MAXPOS
        row_start = (device // N_TX * TILE + offsets[0, slot_index]).astype(jnp.int32)
        col_start = (device % N_TX * TILE + offsets[1, slot_index]).astype(jnp.int32)
        corner = (anchor, anchor, row_start, col_start)
        window = lax.dynamic_slice(object_field, corner, (SLICES, 2, PATCH, PATCH))
        pieces, probe_piece = patch_gradient(window, probe_wave, prop_real, prop_imag, amplitude[slot_index], cosine, sine_table)
        weight = live_slots[slot_index].astype(jnp.float32)
        previous = lax.dynamic_slice(gradient, corner, (SLICES, 2, PATCH, PATCH))
        gradient = lax.dynamic_update_slice(gradient, previous + weight * pieces, corner)
        return ((gradient, probe_total + weight * probe_piece), None)
    initial = (jnp.zeros(object_field.shape, jnp.float32), jnp.zeros(probe_wave.shape, jnp.float32))
    (gradient, probe_total), ignored = lax.scan(visit, initial, jnp.arange(MAXPOS * N_TY * N_TX, dtype=jnp.int32))
    return (gradient, probe_total * (1.0 / math.sqrt(MAXPOS * N_TY * N_TX)))
```

```python
import functools
import math

import jax
import jax.numpy as jnp
import ml_dtypes
import numpy as np
from jax import lax
from jax.experimental import pallas as pl
from jax.experimental.pallas import tpu as pltpu
from jax.sharding import PartitionSpec as P

F32 = jnp.float32
BF16 = jnp.bfloat16
MESH = pl.DeviceIdType.MESH
LANES = 128
INNER = 4


def halves(table):
    high = table.astype(np.float32).astype(ml_dtypes.bfloat16)
    low = (table - high.astype(np.float64)).astype(ml_dtypes.bfloat16)
    return np.stack([high, low])


def dft_halves(length):
    half = length // 2
    sample = np.arange(half)[:, None]
    tables = []
    for parity in range(2):
        freq = 2 * np.arange(half)[None, :] + parity
        angle = 2.0 * math.pi * ((sample * freq) % length) / length
        cosine = np.cos(angle) / math.sqrt(length)
        sine = np.sin(angle) / math.sqrt(length)
        full = np.block([[cosine, -sine], [sine, cosine]])
        tables.append(np.stack([halves(full), halves(full.T)]))
    return np.stack(tables)


def even_odd(length):
    order = np.concatenate([np.arange(0, length, 2), np.arange(1, length, 2)])
    chosen = np.zeros((length, length), np.float32)
    chosen[order, np.arange(length)] = 1.0
    return np.stack([chosen, chosen.T]).astype(ml_dtypes.bfloat16)


def split(value):
    high = value.astype(BF16)
    low = (value - high.astype(F32)).astype(BF16)
    return high, low


def product(left, right):
    return jnp.dot(left, right, preferred_element_type=F32)


def from_right(value, table):
    high, low = split(value)
    left = jnp.concatenate([high, low, high], axis=1)
    return product(left, jnp.concatenate([table[0], table[0], table[1]], axis=0))


def from_left(table, value):
    high, low = split(value)
    right = jnp.concatenate([high, low, high], axis=0)
    return product(jnp.concatenate([table[0], table[0], table[1]], axis=1), right)


def thirds(value):
    high = value.astype(BF16)
    rest = value - high.astype(F32)
    middle = rest.astype(BF16)
    low = (rest - middle.astype(F32)).astype(BF16)
    return high, middle, low


def reorder(value, chosen, chosen_t):
    pieces = thirds(value)
    across = sum(product(piece, chosen) for piece in pieces)
    return sum(product(chosen_t, piece) for piece in thirds(across))


def beside(left, right):
    return jnp.concatenate([left, right], axis=1)


def above(top, bottom):
    return jnp.concatenate([top, bottom], axis=0)


def forward(real, imag, tables):
    n = LANES
    even = from_right(
        beside(real[:, :n] + real[:, n:], imag[:, :n] + imag[:, n:]), tables[0, 0]
    )
    odd = from_right(
        beside(real[:, :n] - real[:, n:], imag[:, :n] - imag[:, n:]), tables[1, 0]
    )
    real = beside(even[:, :n], odd[:, :n])
    imag = beside(even[:, n:], odd[:, n:])
    even = from_left(tables[0, 1], above(real[:n] + real[n:], imag[:n] + imag[n:]))
    odd = from_left(tables[1, 1], above(real[:n] - real[n:], imag[:n] - imag[n:]))
    return above(even[:n], odd[:n]), above(even[n:], odd[n:])


def backward(real, imag, tables):
    n = LANES
    even = from_left(tables[0, 0], above(real[:n], imag[:n]))
    odd = from_left(tables[1, 0], above(real[n:], imag[n:]))
    total, change = even + odd, even - odd
    real, imag = above(total[:n], change[:n]), above(total[n:], change[n:])
    even = from_right(beside(real[:, :n], imag[:, :n]), tables[0, 1])
    odd = from_right(beside(real[:, n:], imag[:, n:]), tables[1, 1])
    total, change = even + odd, even - odd
    return beside(total[:, :n], change[:, :n]), beside(total[:, n:], change[:, n:])


def step_kernel(
    n_ty,
    n_tx,
    obj,
    probe,
    phase,
    amplitude,
    offsets,
    live,
    tables,
    chosen,
    grad,
    probe_grad,
    wide_first,
    wide_second,
    padded,
    total,
    from_left_tile,
    from_above,
    psi,
    trans,
    prop,
    target,
    local_sem,
    get_send,
    get_recv,
    put_send,
    put_recv,
    out_sem,
):
    wide = (wide_first, wide_second)
    layers, _, tile, _ = obj.shape
    patch = probe.shape[1]
    slots = amplitude.shape[0]
    lane_tiles = tile // LANES
    strip_tiles = patch // LANES
    all_tiles = lane_tiles + strip_tiles
    lower = tile - patch
    ty, tx = lax.axis_index("ty"), lax.axis_index("tx")
    left = (ty, lax.rem(tx + n_tx - 1, n_tx))
    right = (ty, lax.rem(tx + 1, n_tx))
    up = (lax.rem(ty + n_ty - 1, n_ty), tx)
    down = (lax.rem(ty + 1, n_ty), tx)

    barrier = pltpu.get_barrier_semaphore()
    for neighbour in (left, right, up, down):
        pl.semaphore_signal(barrier, inc=1, device_id=neighbour, device_id_type=MESH)
    pl.semaphore_wait(barrier, 4)

    def remote(source, destination, send, recv, device):
        return pltpu.make_async_remote_copy(
            src_ref=source,
            dst_ref=destination,
            send_sem=send,
            recv_sem=recv,
            device_id=device,
            device_id_type=MESH,
        )

    def columns(j):
        return pl.ds(j * LANES, LANES)

    def get(s, source, destination, index, device):
        return remote(source, destination, get_send.at[s, index], get_recv.at[s, index], device)

    def get_right(s, block):
        first, size = ((0, patch), (patch, lower))[block]
        return [
            get(
                s,
                obj.at[s, :, pl.ds(first, size), columns(j)],
                wide[s].at[:, lane_tiles + j, pl.ds(first, size), :],
                block * strip_tiles + j,
                left,
            )
            for j in range(strip_tiles)
        ]

    def get_below(s):
        return [
            get(
                s,
                obj.at[s, :, pl.ds(0, patch), columns(j)],
                wide[s].at[:, j, pl.ds(tile, patch), :],
                2 * strip_tiles + j,
                up,
            )
            for j in range(lane_tiles)
        ]

    def get_corner(s):
        corner = pl.ds(lane_tiles, strip_tiles)
        return get(
            s,
            wide[s].at[:, corner, pl.ds(0, patch), :],
            wide[s].at[:, corner, pl.ds(tile, patch), :],
            2 * strip_tiles + lane_tiles,
            up,
        )

    def start_get(s):
        for copy in get_right(s, 0) + get_below(s) + get_right(s, 1):
            copy.start()

    def relay_get(s):
        for copy in get_right(s, 0):
            copy.wait_recv()
        get_corner(s).start()

    def finish_get(s):
        for copy in get_right(s, 1) + get_below(s) + [get_corner(s)]:
            copy.wait_recv()

    def sent_get(s):
        for copy in get_right(s, 0) + get_right(s, 1) + get_below(s) + [get_corner(s)]:
            copy.wait_send()

    def put(s, source, destination, index, device):
        return remote(source, destination, put_send.at[s, index], put_recv.at[s, index], device)

    def put_rows(s, first, size, index):
        return put(
            s,
            total.at[s, :, pl.ds(lane_tiles, strip_tiles), pl.ds(first, size), :],
            from_left_tile.at[s, :, :, pl.ds(first, size), :],
            index,
            right,
        )

    def put_below(s, first, count, index):
        return put(
            s,
            total.at[s, :, pl.ds(first, count), pl.ds(tile, patch), :],
            from_above.at[s, :, pl.ds(first, count), :, :],
            index,
            down,
        )

    def put_part(s, index):
        if index == 0:
            return put_below(s, lane_tiles, strip_tiles, index)
        if index == 1:
            return put_rows(s, patch, lower, index)
        if index == 2:
            return put_below(s, 0, lane_tiles, index)
        return put_rows(s, 0, patch, index)

    def start_put(s):
        for index in range(3):
            put_part(s, index).start()

    def relay_put(s):
        put_part(s, 0).wait_recv()

        def add_rows(block, carry):
            rows = pl.ds(pl.multiple_of(block * 64, 64), 64)
            for part in range(2):
                for j in range(lane_tiles, all_tiles):
                    total[s, part, j, rows, :] += from_above[s, part, j, rows, :]
            return carry

        lax.fori_loop(0, patch // 64, add_rows, 0)
        put_part(s, 3).start()

    def out_copies(s):
        return [
            pltpu.make_async_copy(
                total.at[s, :, j, pl.ds(0, tile), :],
                grad.at[s, :, :, columns(j)],
                out_sem.at[s, j],
            )
            for j in range(lane_tiles)
        ]

    def finish_put(s):
        for index in range(1, 4):
            put_part(s, index).wait_recv()

        def add_rows(block, carry):
            rows = pl.ds(pl.multiple_of(block * 64, 64), 64)
            for part in range(2):
                for j in range(strip_tiles):
                    total[s, part, j, rows, :] += from_left_tile[s, part, j, rows, :]
            return carry

        def add_above(block, carry):
            rows = pl.ds(pl.multiple_of(block * 64, 64), 64)
            for part in range(2):
                for j in range(lane_tiles):
                    total[s, part, j, rows, :] += from_above[s, part, j, rows, :]
            return carry

        lax.fori_loop(0, tile // 64, add_rows, 0)
        lax.fori_loop(0, patch // 64, add_above, 0)
        for copy in out_copies(s):
            copy.start()

    start_get(0)
    local = [
        pltpu.make_async_copy(
            obj.at[s, :, :, columns(j)], wide[s].at[:, j, pl.ds(0, tile), :], local_sem.at[s, j]
        )
        for s in range(layers)
        for j in range(lane_tiles)
    ]
    for copy in local:
        copy.start()

    def clear(q, carry):
        for part in range(2):
            for j in range(strip_tiles + 1):
                padded[q, part, j, pl.ds(0, tile), :] = jnp.zeros((tile, LANES), F32)
                padded[q, part, j, pl.ds(tile + patch, tile), :] = jnp.zeros((tile, LANES), F32)
        return carry

    lax.fori_loop(0, slots, clear, 0)

    def order_target(q, carry):
        target[q] = reorder(amplitude[q], chosen[0], chosen[1])
        return carry

    lax.fori_loop(0, slots, order_target, 0)
    angle = reorder(phase[...], chosen[0], chosen[1])
    prop[0] = jnp.cos(angle)
    prop[1] = jnp.sin(angle)
    for copy in local:
        copy.wait()
    relay_get(0)
    finish_get(0)
    sent_get(0)
    start_get(1)

    lane = lax.broadcasted_iota(jnp.int32, (patch, LANES), 1)

    def place(q):
        row, column = offsets[0, q], offsets[1, q]
        return row, lax.shift_right_logical(column, 7), lax.bitwise_and(column, LANES - 1)

    def window(s, part, q):
        row, tile_index, shift = place(q)
        back = lax.bitwise_and(LANES - shift, LANES - 1)
        rolled = [
            pltpu.roll(wide[s][part, tile_index + k, pl.ds(row, patch), :], back, 1)
            for k in range(strip_tiles + 1)
        ]
        keep = lane < LANES - shift
        return jnp.concatenate(
            [jnp.where(keep, rolled[k], rolled[k + 1]) for k in range(strip_tiles)], axis=1
        )

    def deposit(q, part, piece):
        _, _, shift = place(q)
        rolled = [
            pltpu.roll(piece[:, k * LANES : (k + 1) * LANES], shift, 1) for k in range(strip_tiles)
        ]
        rolled = [jnp.zeros((patch, LANES), F32)] + rolled + [jnp.zeros((patch, LANES), F32)]
        keep = lane >= shift
        for k in range(strip_tiles + 1):
            padded[q, part, k, pl.ds(tile, patch), :] = jnp.where(keep, rolled[k + 1], rolled[k])

    def gather(s, tiles, first, size):
        places = [place(q) for q in range(slots)]
        alive = [live[q].astype(F32) for q in range(slots)]

        def rows_of(block, carry):
            begin = first + block * 64
            for j in tiles:
                weights, sources = [], []
                for q in range(slots):
                    inside = j - places[q][1]
                    valid = jnp.logical_and(inside >= 0, inside <= strip_tiles)
                    weights.append(jnp.where(valid, alive[q], 0.0))
                    sources.append(jnp.clip(inside, 0, strip_tiles))
                for part in range(2):
                    value = jnp.zeros((64, LANES), F32)
                    for q in range(slots):
                        rows = pl.ds(tile - places[q][0] + begin, 64)
                        value += weights[q] * padded[q, part, sources[q], rows, :]
                    total[s, part, j, pl.ds(pl.multiple_of(begin, 64), 64), :] = value
            return carry

        lax.fori_loop(0, size // 64, rows_of, 0)

    def first_layer(q, carry):
        trans_real, trans_imag = window(0, 0, q), window(0, 1, q)
        trans[q, 0], trans[q, 1] = trans_real, trans_imag
        freq_real, freq_imag = forward(
            trans_real * probe[0] - trans_imag * probe[1],
            trans_real * probe[1] + trans_imag * probe[0],
            tables,
        )
        psi[q, 0], psi[q, 1] = backward(
            prop[0] * freq_real - prop[1] * freq_imag,
            prop[0] * freq_imag + prop[1] * freq_real,
            tables,
        )
        return carry

    lax.fori_loop(0, slots, first_layer, 0)
    relay_get(1)
    finish_get(1)
    sent_get(1)

    def second_layer(q, carry):
        trans_real, trans_imag = window(1, 0, q), window(1, 1, q)
        wave_real, wave_imag = psi[q, 0], psi[q, 1]
        freq_real, freq_imag = forward(
            trans_real * wave_real - trans_imag * wave_imag,
            trans_real * wave_imag + trans_imag * wave_real,
            tables,
        )
        energy = freq_real * freq_real + freq_imag * freq_imag + 0.25
        factor = target[q] / jnp.sqrt(energy) - 1.0
        back_real, back_imag = backward(freq_real * factor, freq_imag * factor, tables)
        wave_real, wave_imag = psi[q, 0], psi[q, 1]
        deposit(q, 0, wave_real * back_real + wave_imag * back_imag)
        deposit(q, 1, wave_real * back_imag - wave_imag * back_real)
        trans_real, trans_imag = window(1, 0, q), window(1, 1, q)
        psi[q, 0] = trans_real * back_real + trans_imag * back_imag
        psi[q, 1] = trans_real * back_imag - trans_imag * back_real
        return carry

    lax.fori_loop(0, slots, second_layer, 0)
    strip = range(lane_tiles, all_tiles)
    inner = range(lane_tiles)

    def send_edges(s):
        gather(s, strip, 0, tile + patch)
        gather(s, inner, tile, patch)
        start_put(s)
        gather(s, inner, 0, tile)

    send_edges(1)
    probe_grad[...] = jnp.zeros(probe_grad.shape, F32)

    def third_layer(q, carry):
        freq_real, freq_imag = forward(psi[q, 0], psi[q, 1], tables)
        back_real, back_imag = backward(
            prop[0] * freq_real + prop[1] * freq_imag,
            prop[0] * freq_imag - prop[1] * freq_real,
            tables,
        )
        deposit(q, 0, probe[0] * back_real + probe[1] * back_imag)
        deposit(q, 1, probe[0] * back_imag - probe[1] * back_real)
        weight = live[q].astype(F32)
        probe_grad[0] += weight * (trans[q, 0] * back_real + trans[q, 1] * back_imag)
        probe_grad[1] += weight * (trans[q, 0] * back_imag - trans[q, 1] * back_real)
        return carry

    lax.fori_loop(0, slots // 2, third_layer, 0)
    relay_put(1)
    lax.fori_loop(slots // 2, slots, third_layer, 0)
    send_edges(0)
    finish_put(1)
    relay_put(0)
    finish_put(0)
    for s in range(layers):
        for index in range(4):
            put_part(s, index).wait_send()
        for copy in out_copies(s):
            copy.wait()


def step_call(n_ty, n_tx, *operands):
    obj, probe, _, amplitude, _, _, _, _ = operands
    layers, _, tile, _ = obj.shape
    patch = probe.shape[1]
    slots = amplitude.shape[0]
    lane_tiles, strip_tiles = tile // LANES, patch // LANES
    all_tiles = lane_tiles + strip_tiles
    gets = 2 * strip_tiles + lane_tiles + 1
    vmem = pl.BlockSpec(memory_space=pltpu.VMEM)
    smem = pl.BlockSpec(memory_space=pltpu.SMEM)
    whole = pl.BlockSpec(memory_space=pl.ANY)
    return pl.pallas_call(
        functools.partial(step_kernel, n_ty, n_tx),
        name="step",
        out_shape=(
            jax.ShapeDtypeStruct(obj.shape, F32),
            jax.ShapeDtypeStruct(probe.shape, F32),
        ),
        in_specs=[whole, vmem, vmem, vmem, smem, smem, vmem, vmem],
        out_specs=(whole, vmem),
        scratch_shapes=[
            pltpu.VMEM((2, all_tiles, tile + patch, LANES), F32),
            pltpu.VMEM((2, all_tiles, tile + patch, LANES), F32),
            pltpu.VMEM((slots, 2, strip_tiles + 1, 2 * tile + patch, LANES), F32),
            pltpu.VMEM((layers, 2, all_tiles, tile + patch, LANES), F32),
            pltpu.VMEM((layers, 2, strip_tiles, tile, LANES), F32),
            pltpu.VMEM((layers, 2, all_tiles, patch, LANES), F32),
            pltpu.VMEM((slots, 2, patch, patch), F32),
            pltpu.VMEM((slots, 2, patch, patch), F32),
            pltpu.VMEM((2, patch, patch), F32),
            pltpu.VMEM((slots, patch, patch), F32),
            pltpu.SemaphoreType.DMA((layers, lane_tiles)),
            pltpu.SemaphoreType.DMA((layers, gets)),
            pltpu.SemaphoreType.DMA((layers, gets)),
            pltpu.SemaphoreType.DMA((layers, 4)),
            pltpu.SemaphoreType.DMA((layers, 4)),
            pltpu.SemaphoreType.DMA((layers, lane_tiles)),
        ],
        compiler_params=pltpu.CompilerParams(
            collective_id=0, has_side_effects=True, vmem_limit_bytes=60 * 1024 * 1024
        ),
    )(*operands)


def sum_kernel(
    n_ty, n_tx, scaling, part, whole, near, far, near_send, near_recv, far_send, far_recv,
    last_send, last_recv,
):
    near_count, far_count = n_ty * INNER, n_tx // INNER
    ty, tx = lax.axis_index("ty"), lax.axis_index("tx")
    inner, outer = lax.rem(tx, INNER), lax.div(tx, INNER)
    mine = ty * INNER + inner

    def near_peer(step):
        index = lax.rem(mine + step, near_count)
        return index, (lax.div(index, INNER), outer * INNER + lax.rem(index, INNER))

    def far_peer(step):
        index = lax.rem(outer + step, far_count)
        return index, (ty, index * INNER + inner)

    barrier = pltpu.get_barrier_semaphore()

    def greet_near(step, carry):
        pl.semaphore_signal(barrier, inc=1, device_id=near_peer(step)[1], device_id_type=MESH)
        return carry

    def greet_far(step, carry):
        pl.semaphore_signal(barrier, inc=1, device_id=far_peer(step)[1], device_id_type=MESH)
        return carry

    lax.fori_loop(1, near_count, greet_near, 0)
    lax.fori_loop(1, far_count, greet_far, 0)
    pl.semaphore_wait(barrier, near_count + far_count - 2)

    def remote(source, destination, send, recv, device):
        return pltpu.make_async_remote_copy(
            src_ref=source,
            dst_ref=destination,
            send_sem=send,
            recv_sem=recv,
            device_id=device,
            device_id_type=MESH,
        )

    def exchange(count, peer, make):
        def start(step, carry):
            make(*peer(step))[0].start()
            return carry

        def wait(step, carry):
            make(*peer(step))[1].wait_recv()
            return carry

        def sent(step, carry):
            make(*peer(step))[0].wait_send()
            return carry

        lax.fori_loop(1, count, start, 0)
        lax.fori_loop(1, count, wait, 0)
        return lambda: lax.fori_loop(1, count, sent, 0)

    def scatter(index, device):
        return (
            remote(part.at[index], near.at[mine], near_send.at[index], near_recv.at[mine], device),
            remote(part.at[mine], near.at[index], near_send.at[index], near_recv.at[index], device),
        )

    near[mine] = part[mine]
    done_near = exchange(near_count, near_peer, scatter)
    value = near[0]
    for index in range(1, near_count):
        value += near[index]
    far[outer] = value

    def across(index, device):
        return (
            remote(far.at[outer], far.at[outer], far_send.at[index], far_recv.at[outer], device),
            remote(far.at[outer], far.at[index], far_send.at[index], far_recv.at[index], device),
        )

    done_far = exchange(far_count, far_peer, across)
    value = far[0]
    for index in range(1, far_count):
        value += far[index]
    whole[mine] = value * scaling

    def spread(index, device):
        return (
            remote(
                whole.at[mine], whole.at[mine], last_send.at[index], last_recv.at[mine], device
            ),
            remote(
                whole.at[mine], whole.at[index], last_send.at[index], last_recv.at[index], device
            ),
        )

    done_last = exchange(near_count, near_peer, spread)
    done_near()
    done_far()
    done_last()


def sum_call(n_ty, n_tx, scaling, value):
    near_count, far_count = n_ty * INNER, n_tx // INNER
    width = value.shape[-1]
    rows = value.size // width // near_count
    vmem = pl.BlockSpec(memory_space=pltpu.VMEM)
    sems = pltpu.SemaphoreType.DMA
    summed = pl.pallas_call(
        functools.partial(sum_kernel, n_ty, n_tx, scaling),
        name="sum_probe",
        out_shape=jax.ShapeDtypeStruct((near_count, rows, width), F32),
        in_specs=[vmem],
        out_specs=vmem,
        scratch_shapes=[
            pltpu.VMEM((near_count, rows, width), F32),
            pltpu.VMEM((far_count, rows, width), F32),
            sems((near_count,)),
            sems((near_count,)),
            sems((far_count,)),
            sems((far_count,)),
            sems((near_count,)),
            sems((near_count,)),
        ],
        compiler_params=pltpu.CompilerParams(collective_id=1, has_side_effects=True),
    )(value.reshape(near_count, rows, width))
    return summed.reshape(value.shape)


def solution(mesh):
    n_ty, n_tx = mesh.shape["ty"], mesh.shape["tx"]

    def per_device(object_field, probe_wave, prop_phase, amplitude, offsets, live_slots):
        patch = probe_wave.shape[1]
        owned, probe_part = step_call(
            n_ty,
            n_tx,
            object_field,
            probe_wave,
            prop_phase,
            amplitude,
            offsets,
            live_slots,
            jnp.asarray(dft_halves(patch)),
            jnp.asarray(even_odd(patch)),
        )
        scaling = 1.0 / math.sqrt(live_slots.shape[0] * n_ty * n_tx)
        return owned, sum_call(n_ty, n_tx, scaling, probe_part)

    placed = (
        P(None, None, "ty", "tx"),
        P(),
        P(),
        P(("ty", "tx"), None, None),
        P(None, ("ty", "tx")),
        P(("ty", "tx")),
    )
    return jax.shard_map(
        per_device,
        mesh=mesh,
        in_specs=placed,
        out_specs=(P(None, None, "ty", "tx"), P()),
        check_vma=False,
    )
```

```python
import functools
import math

import jax
import jax.numpy as jnp
import ml_dtypes
import numpy as np
from jax import lax
from jax.experimental import pallas as pl
from jax.experimental.pallas import tpu as pltpu
from jax.sharding import PartitionSpec as P

F32 = jnp.float32
BF16 = jnp.bfloat16
MESH = pl.DeviceIdType.MESH
LANES = 128
INNER = 4


def halves(table):
    high = table.astype(np.float32).astype(ml_dtypes.bfloat16)
    low = (table - high.astype(np.float64)).astype(ml_dtypes.bfloat16)
    return np.stack([high, low])


def dft_halves(length):
    half = length // 2
    sample = np.arange(half)[:, None]
    tables = []
    for parity in range(2):
        freq = 2 * np.arange(half)[None, :] + parity
        angle = 2.0 * math.pi * ((sample * freq) % length) / length
        cosine = np.cos(angle) / math.sqrt(length)
        sine = np.sin(angle) / math.sqrt(length)
        full = np.block([[cosine, -sine], [sine, cosine]])
        tables.append(np.stack([halves(full), halves(full.T)]))
    return np.stack(tables)


def even_odd(length):
    order = np.concatenate([np.arange(0, length, 2), np.arange(1, length, 2)])
    chosen = np.zeros((length, length), np.float32)
    chosen[order, np.arange(length)] = 1.0
    return np.stack([chosen, chosen.T]).astype(ml_dtypes.bfloat16)


def split(value):
    high = value.astype(BF16)
    low = (value - high.astype(F32)).astype(BF16)
    return high, low


def product(left, right):
    return jnp.dot(left, right, preferred_element_type=F32)


def from_right(value, table):
    high, low = split(value)
    left = jnp.concatenate([high, low, high], axis=1)
    return product(left, jnp.concatenate([table[0], table[0], table[1]], axis=0))


def from_left(table, value):
    high, low = split(value)
    right = jnp.concatenate([high, low, high], axis=0)
    return product(jnp.concatenate([table[0], table[0], table[1]], axis=1), right)


def thirds(value):
    high = value.astype(BF16)
    rest = value - high.astype(F32)
    middle = rest.astype(BF16)
    low = (rest - middle.astype(F32)).astype(BF16)
    return high, middle, low


def reorder(value, chosen, chosen_t):
    pieces = thirds(value)
    across = sum(product(piece, chosen) for piece in pieces)
    return sum(product(chosen_t, piece) for piece in thirds(across))


def beside(left, right):
    return jnp.concatenate([left, right], axis=1)


def above(top, bottom):
    return jnp.concatenate([top, bottom], axis=0)


def forward(real, imag, tables):
    n = LANES
    even = from_right(
        beside(real[:, :n] + real[:, n:], imag[:, :n] + imag[:, n:]), tables[0, 0]
    )
    odd = from_right(
        beside(real[:, :n] - real[:, n:], imag[:, :n] - imag[:, n:]), tables[1, 0]
    )
    real = beside(even[:, :n], odd[:, :n])
    imag = beside(even[:, n:], odd[:, n:])
    even = from_left(tables[0, 1], above(real[:n] + real[n:], imag[:n] + imag[n:]))
    odd = from_left(tables[1, 1], above(real[:n] - real[n:], imag[:n] - imag[n:]))
    return above(even[:n], odd[:n]), above(even[n:], odd[n:])


def backward(real, imag, tables):
    n = LANES
    even = from_left(tables[0, 0], above(real[:n], imag[:n]))
    odd = from_left(tables[1, 0], above(real[n:], imag[n:]))
    total, change = even + odd, even - odd
    real, imag = above(total[:n], change[:n]), above(total[n:], change[n:])
    even = from_right(beside(real[:, :n], imag[:, :n]), tables[0, 1])
    odd = from_right(beside(real[:, n:], imag[:, n:]), tables[1, 1])
    total, change = even + odd, even - odd
    return beside(total[:, :n], change[:, :n]), beside(total[:, n:], change[:, n:])


def step_kernel(
    n_ty,
    n_tx,
    scaling,
    obj,
    probe,
    phase,
    amplitude,
    offsets,
    live,
    tables,
    chosen,
    grad,
    probe_grad,
    wide_first,
    wide_second,
    padded,
    total,
    from_left_tile,
    from_above,
    psi,
    trans,
    prop,
    target,
    probe_part,
    pair_part,
    layer_part,
    outer_part,
    inner_chunks,
    inner_part,
    row_part,
    local_sem,
    get_send,
    get_recv,
    put_send,
    put_recv,
    out_sem,
    sum_send,
    sum_recv,
):
    wide = (wide_first, wide_second)
    layers, _, tile, _ = obj.shape
    patch = probe.shape[1]
    slots = amplitude.shape[0]
    lane_tiles = tile // LANES
    strip_tiles = patch // LANES
    all_tiles = lane_tiles + strip_tiles
    lower = tile - patch
    ty, tx = lax.axis_index("ty"), lax.axis_index("tx")
    left = (ty, lax.rem(tx + n_tx - 1, n_tx))
    right = (ty, lax.rem(tx + 1, n_tx))
    up = (lax.rem(ty + n_ty - 1, n_ty), tx)
    down = (lax.rem(ty + 1, n_ty), tx)

    n_row, n_outer = n_ty // 2, n_tx // INNER
    core, row = lax.rem(ty, 2), lax.div(ty, 2)
    inner, outer = lax.rem(tx, INNER), lax.div(tx, INNER)
    partner = (ty + 1 - 2 * core, tx)

    def outer_peer(step):
        index = lax.rem(outer + step, n_outer)
        return index, (ty, index * INNER + inner)

    def inner_peer(step):
        index = lax.rem(inner + step, INNER)
        return index, (ty, outer * INNER + index)

    def row_peer(step):
        index = lax.rem(row + step, n_row)
        return index, (index * 2 + core, tx)

    barrier = pltpu.get_barrier_semaphore()
    greeted = [left, right, up, down, partner]
    greeted += [outer_peer(step)[1] for step in range(1, n_outer)]
    greeted += [inner_peer(step)[1] for step in range(1, INNER)]
    greeted += [row_peer(step)[1] for step in range(1, n_row)]
    for device in greeted:
        pl.semaphore_signal(barrier, inc=1, device_id=device, device_id_type=MESH)
    pl.semaphore_wait(barrier, len(greeted))

    def remote(source, destination, send, recv, device):
        return pltpu.make_async_remote_copy(
            src_ref=source,
            dst_ref=destination,
            send_sem=send,
            recv_sem=recv,
            device_id=device,
            device_id_type=MESH,
        )

    def columns(j):
        return pl.ds(j * LANES, LANES)

    def get(s, source, destination, index, device):
        return remote(source, destination, get_send.at[s, index], get_recv.at[s, index], device)

    def get_right(s, block):
        first, size = ((0, patch), (patch, lower))[block]
        return [
            get(
                s,
                obj.at[s, :, pl.ds(first, size), columns(j)],
                wide[s].at[:, lane_tiles + j, pl.ds(first, size), :],
                block * strip_tiles + j,
                left,
            )
            for j in range(strip_tiles)
        ]

    def get_below(s):
        return [
            get(
                s,
                obj.at[s, :, pl.ds(0, patch), columns(j)],
                wide[s].at[:, j, pl.ds(tile, patch), :],
                2 * strip_tiles + j,
                up,
            )
            for j in range(lane_tiles)
        ]

    def get_corner(s, j):
        return get(
            s,
            wide[s].at[:, lane_tiles + j, pl.ds(0, patch), :],
            wide[s].at[:, lane_tiles + j, pl.ds(tile, patch), :],
            2 * strip_tiles + lane_tiles + j,
            up,
        )

    def start_get(s):
        for copy in get_right(s, 0) + get_below(s) + get_right(s, 1):
            copy.start()

    def relay_get(s):
        for j, copy in enumerate(get_right(s, 0)):
            copy.wait_recv()
            get_corner(s, j).start()

    def finish_get(s):
        for copy in get_right(s, 1) + get_below(s):
            copy.wait_recv()
        for j in range(strip_tiles):
            get_corner(s, j).wait_recv()

    def sent_get(s):
        for copy in get_right(s, 0) + get_right(s, 1) + get_below(s):
            copy.wait_send()

    def sent_corner(s):
        for j in range(strip_tiles):
            get_corner(s, j).wait_send()

    def put(s, source, destination, index, device):
        return remote(source, destination, put_send.at[s, index], put_recv.at[s, index], device)

    def put_corner(s, j):
        return put(
            s,
            total.at[s, :, lane_tiles + j, pl.ds(tile, patch), :],
            from_above.at[s, :, lane_tiles + j, :, :],
            j,
            down,
        )

    def put_top(s, j):
        return put(
            s,
            total.at[s, :, lane_tiles + j, pl.ds(0, patch), :],
            from_left_tile.at[s, :, j, pl.ds(0, patch), :],
            strip_tiles + j,
            right,
        )

    def put_bottom(s):
        return put(
            s,
            total.at[s, :, pl.ds(lane_tiles, strip_tiles), pl.ds(patch, lower), :],
            from_left_tile.at[s, :, :, pl.ds(patch, lower), :],
            2 * strip_tiles,
            right,
        )

    def put_below(s):
        return put(
            s,
            total.at[s, :, pl.ds(0, lane_tiles), pl.ds(tile, patch), :],
            from_above.at[s, :, pl.ds(0, lane_tiles), :, :],
            2 * strip_tiles + 1,
            down,
        )

    def start_put(s):
        for j in range(strip_tiles):
            put_corner(s, j).start()
        put_bottom(s).start()
        put_below(s).start()

    def relay_put(s):
        for j in range(strip_tiles):
            put_corner(s, j).wait_recv()

            def add_rows(block, carry):
                rows = pl.ds(pl.multiple_of(block * 64, 64), 64)
                for part in range(2):
                    total[s, part, lane_tiles + j, rows, :] += from_above[
                        s, part, lane_tiles + j, rows, :
                    ]
                return carry

            lax.fori_loop(0, patch // 64, add_rows, 0)
            put_top(s, j).start()

    def out_copies(s):
        return [
            pltpu.make_async_copy(
                total.at[s, :, j, pl.ds(0, tile), :],
                grad.at[s, :, :, columns(j)],
                out_sem.at[s, j],
            )
            for j in range(lane_tiles)
        ]

    def finish_put(s):
        put_bottom(s).wait_recv()
        put_below(s).wait_recv()
        for j in range(strip_tiles):
            put_top(s, j).wait_recv()

        def add_rows(block, carry):
            rows = pl.ds(pl.multiple_of(block * 64, 64), 64)
            for part in range(2):
                for j in range(strip_tiles):
                    total[s, part, j, rows, :] += from_left_tile[s, part, j, rows, :]
            return carry

        def add_above(block, carry):
            rows = pl.ds(pl.multiple_of(block * 64, 64), 64)
            for part in range(2):
                for j in range(lane_tiles):
                    total[s, part, j, rows, :] += from_above[s, part, j, rows, :]
            return carry

        lax.fori_loop(0, tile // 64, add_rows, 0)
        lax.fori_loop(0, patch // 64, add_above, 0)
        for copy in out_copies(s):
            copy.start()

    def summed(source, destination, index, device):
        return remote(source, destination, sum_send.at[index], sum_recv.at[index], device)

    first_outer = 1
    first_inner = first_outer + n_outer
    first_row = first_inner + INNER
    second_inner = first_row + n_row
    second_outer = second_inner + INNER
    last_pair = second_outer + n_outer

    def stage(count, peer, base, mine, source, target_of):
        def sending(step):
            index, device = peer(step)
            return remote(
                source(index),
                target_of(mine),
                sum_send.at[base + index],
                sum_recv.at[base + mine],
                device,
            )

        def receiving(step):
            index, device = peer(step)
            return remote(
                source(index),
                target_of(index),
                sum_send.at[base + index],
                sum_recv.at[base + index],
                device,
            )

        def start():
            for step in range(1, count):
                sending(step).start()

        def finish():
            for step in range(1, count):
                receiving(step).wait_recv()

        def sent():
            for step in range(1, count):
                sending(step).wait_send()

        return start, finish, sent

    def pair_sum():
        return summed(probe_part.at[1 - core], pair_part, 0, partner)

    def pair_gather():
        return summed(probe_grad.at[core], probe_grad.at[core], last_pair, partner)

    def pair_arrival():
        return summed(probe_grad.at[1 - core], probe_grad.at[1 - core], last_pair, partner)

    outer_sum = stage(
        n_outer, outer_peer, first_outer, outer,
        lambda index: layer_part.at[index], lambda index: outer_part.at[index],
    )
    inner_sum = stage(
        INNER, inner_peer, first_inner, inner,
        lambda index: inner_chunks.at[index], lambda index: inner_part.at[index],
    )
    row_sum = stage(
        n_row, row_peer, first_row, row,
        lambda index: row_part.at[row], lambda index: row_part.at[index],
    )
    inner_gather = stage(
        INNER, inner_peer, second_inner, inner,
        lambda index: probe_grad.at[core, outer, inner],
        lambda index: probe_grad.at[core, outer, index],
    )
    outer_gather = stage(
        n_outer, outer_peer, second_outer, outer,
        lambda index: probe_grad.at[core, outer],
        lambda index: probe_grad.at[core, index],
    )

    def after_pair():
        pair_sum().wait_recv()
        for index in range(n_outer):
            rows = pl.ds(index * layer_part.shape[1], layer_part.shape[1])
            layer_part[index] = probe_part[core, rows, :] + pair_part[rows, :]
        outer_part[outer] = layer_part[outer]
        outer_sum[0]()

    def after_outer():
        outer_sum[1]()
        size = inner_chunks.shape[1]
        for index in range(INNER):
            rows = pl.ds(index * size, size)
            value = outer_part[0, rows, :]
            for other in range(1, n_outer):
                value += outer_part[other, rows, :]
            inner_chunks[index] = value
        inner_part[inner] = inner_chunks[inner]
        inner_sum[0]()

    def after_inner():
        inner_sum[1]()
        value = inner_part[0]
        for index in range(1, INNER):
            value += inner_part[index]
        row_part[row] = value
        row_sum[0]()

    def after_row():
        row_sum[1]()
        value = row_part[0]
        for index in range(1, n_row):
            value += row_part[index]
        probe_grad[core, outer, inner] = value * scaling
        inner_gather[0]()

    def after_inner_gather():
        inner_gather[1]()
        outer_gather[0]()

    def after_outer_gather():
        outer_gather[1]()
        pair_gather().start()

    def finish_sum():
        pair_arrival().wait_recv()
        pair_gather().wait_send()
        pair_sum().wait_send()
        for part in (outer_sum, inner_sum, row_sum, inner_gather, outer_gather):
            part[2]()

    start_get(0)
    local = [
        pltpu.make_async_copy(
            obj.at[s, :, :, columns(j)], wide[s].at[:, j, pl.ds(0, tile), :], local_sem.at[s, j]
        )
        for s in range(layers)
        for j in range(lane_tiles)
    ]
    for copy in local:
        copy.start()

    def clear(q, carry):
        for part in range(2):
            for j in range(strip_tiles + 1):
                padded[q, part, j, pl.ds(0, tile), :] = jnp.zeros((tile, LANES), F32)
                padded[q, part, j, pl.ds(tile + patch, tile), :] = jnp.zeros((tile, LANES), F32)
        return carry

    lax.fori_loop(0, slots, clear, 0)

    def order_target(q, carry):
        target[q] = reorder(amplitude[q], chosen[0], chosen[1])
        return carry

    lax.fori_loop(0, slots, order_target, 0)
    angle = reorder(phase[...], chosen[0], chosen[1])
    prop[0] = jnp.cos(angle)
    prop[1] = jnp.sin(angle)
    for copy in local:
        copy.wait()
    relay_get(0)
    sent_get(0)
    start_get(1)
    finish_get(0)

    lane = lax.broadcasted_iota(jnp.int32, (patch, LANES), 1)

    def place(q):
        row, column = offsets[0, q], offsets[1, q]
        return row, lax.shift_right_logical(column, 7), lax.bitwise_and(column, LANES - 1)

    def window(s, part, q):
        row, tile_index, shift = place(q)
        back = lax.bitwise_and(LANES - shift, LANES - 1)
        rolled = [
            pltpu.roll(wide[s][part, tile_index + k, pl.ds(row, patch), :], back, 1)
            for k in range(strip_tiles + 1)
        ]
        keep = lane < LANES - shift
        return jnp.concatenate(
            [jnp.where(keep, rolled[k], rolled[k + 1]) for k in range(strip_tiles)], axis=1
        )

    def deposit(q, part, piece):
        _, _, shift = place(q)
        rolled = [
            pltpu.roll(piece[:, k * LANES : (k + 1) * LANES], shift, 1) for k in range(strip_tiles)
        ]
        rolled = [jnp.zeros((patch, LANES), F32)] + rolled + [jnp.zeros((patch, LANES), F32)]
        keep = lane >= shift
        for k in range(strip_tiles + 1):
            padded[q, part, k, pl.ds(tile, patch), :] = jnp.where(keep, rolled[k + 1], rolled[k])

    def gather(s, tiles, first, size):
        places = [place(q) for q in range(slots)]
        alive = [live[q].astype(F32) for q in range(slots)]

        def rows_of(block, carry):
            begin = first + block * 64
            for j in tiles:
                weights, sources = [], []
                for q in range(slots):
                    inside = j - places[q][1]
                    valid = jnp.logical_and(inside >= 0, inside <= strip_tiles)
                    weights.append(jnp.where(valid, alive[q], 0.0))
                    sources.append(jnp.clip(inside, 0, strip_tiles))
                for part in range(2):
                    value = jnp.zeros((64, LANES), F32)
                    for q in range(slots):
                        rows = pl.ds(tile - places[q][0] + begin, 64)
                        value += weights[q] * padded[q, part, sources[q], rows, :]
                    total[s, part, j, pl.ds(pl.multiple_of(begin, 64), 64), :] = value
            return carry

        lax.fori_loop(0, size // 64, rows_of, 0)

    def first_layer(q, carry):
        trans_real, trans_imag = window(0, 0, q), window(0, 1, q)
        trans[q, 0], trans[q, 1] = trans_real, trans_imag
        freq_real, freq_imag = forward(
            trans_real * probe[0] - trans_imag * probe[1],
            trans_real * probe[1] + trans_imag * probe[0],
            tables,
        )
        psi[q, 0], psi[q, 1] = backward(
            prop[0] * freq_real - prop[1] * freq_imag,
            prop[0] * freq_imag + prop[1] * freq_real,
            tables,
        )
        return carry

    lax.fori_loop(0, slots, first_layer, 0)
    sent_corner(0)
    relay_get(1)
    sent_get(1)
    finish_get(1)
    sent_corner(1)

    def second_layer(q, carry):
        trans_real, trans_imag = window(1, 0, q), window(1, 1, q)
        wave_real, wave_imag = psi[q, 0], psi[q, 1]
        freq_real, freq_imag = forward(
            trans_real * wave_real - trans_imag * wave_imag,
            trans_real * wave_imag + trans_imag * wave_real,
            tables,
        )
        energy = freq_real * freq_real + freq_imag * freq_imag + 0.25
        factor = target[q] / jnp.sqrt(energy) - 1.0
        back_real, back_imag = backward(freq_real * factor, freq_imag * factor, tables)
        wave_real, wave_imag = psi[q, 0], psi[q, 1]
        deposit(q, 0, wave_real * back_real + wave_imag * back_imag)
        deposit(q, 1, wave_real * back_imag - wave_imag * back_real)
        trans_real, trans_imag = window(1, 0, q), window(1, 1, q)
        psi[q, 0] = trans_real * back_real + trans_imag * back_imag
        psi[q, 1] = trans_real * back_imag - trans_imag * back_real
        return carry

    lax.fori_loop(0, slots, second_layer, 0)
    strip = range(lane_tiles, all_tiles)
    own = range(lane_tiles)

    def send_edges(s):
        gather(s, strip, 0, tile + patch)
        gather(s, own, tile, patch)
        start_put(s)

    send_edges(1)
    gather(1, own, 0, tile)
    probe_part[...] = jnp.zeros(probe_part.shape, F32)

    def third_layer(q, carry):
        freq_real, freq_imag = forward(psi[q, 0], psi[q, 1], tables)
        back_real, back_imag = backward(
            prop[0] * freq_real + prop[1] * freq_imag,
            prop[0] * freq_imag - prop[1] * freq_real,
            tables,
        )
        deposit(q, 0, probe[0] * back_real + probe[1] * back_imag)
        deposit(q, 1, probe[0] * back_imag - probe[1] * back_real)
        weight = live[q].astype(F32)
        probe_part[0] += weight * (trans[q, 0] * back_real + trans[q, 1] * back_imag)
        probe_part[1] += weight * (trans[q, 0] * back_imag - trans[q, 1] * back_real)
        return carry

    lax.fori_loop(0, slots // 2, third_layer, 0)
    relay_put(1)
    lax.fori_loop(slots // 2, slots, third_layer, 0)
    pair_sum().start()
    send_edges(0)
    after_pair()
    gather(0, own, 0, tile)
    finish_put(1)
    after_outer()
    relay_put(0)
    after_inner()
    after_row()
    after_inner_gather()
    after_outer_gather()
    finish_put(0)
    finish_sum()
    for s in range(layers):
        put_bottom(s).wait_send()
        put_below(s).wait_send()
        for j in range(strip_tiles):
            put_corner(s, j).wait_send()
            put_top(s, j).wait_send()
        for copy in out_copies(s):
            copy.wait()


def step_call(n_ty, n_tx, scaling, *operands):
    obj, probe, _, amplitude, _, _, _, _ = operands
    layers, _, tile, _ = obj.shape
    patch = probe.shape[1]
    slots = amplitude.shape[0]
    lane_tiles, strip_tiles = tile // LANES, patch // LANES
    all_tiles = lane_tiles + strip_tiles
    gets = 3 * strip_tiles + lane_tiles
    puts = 2 * strip_tiles + 2
    n_row, n_outer = n_ty // 2, n_tx // INNER
    layer_rows = patch // n_outer
    chunk = layer_rows // INNER
    sums = 2 * n_outer + 2 * INNER + n_row + 2
    vmem = pl.BlockSpec(memory_space=pltpu.VMEM)
    smem = pl.BlockSpec(memory_space=pltpu.SMEM)
    whole = pl.BlockSpec(memory_space=pl.ANY)
    return pl.pallas_call(
        functools.partial(step_kernel, n_ty, n_tx, scaling),
        name="step",
        out_shape=(
            jax.ShapeDtypeStruct(obj.shape, F32),
            jax.ShapeDtypeStruct((2, n_outer, INNER, chunk, patch), F32),
        ),
        in_specs=[whole, vmem, vmem, vmem, smem, smem, vmem, vmem],
        out_specs=(whole, vmem),
        scratch_shapes=[
            pltpu.VMEM((2, all_tiles, tile + patch, LANES), F32),
            pltpu.VMEM((2, all_tiles, tile + patch, LANES), F32),
            pltpu.VMEM((slots, 2, strip_tiles + 1, 2 * tile + patch, LANES), F32),
            pltpu.VMEM((layers, 2, all_tiles, tile + patch, LANES), F32),
            pltpu.VMEM((layers, 2, strip_tiles, tile, LANES), F32),
            pltpu.VMEM((layers, 2, all_tiles, patch, LANES), F32),
            pltpu.VMEM((slots, 2, patch, patch), F32),
            pltpu.VMEM((slots, 2, patch, patch), F32),
            pltpu.VMEM((2, patch, patch), F32),
            pltpu.VMEM((slots, patch, patch), F32),
            pltpu.VMEM((2, patch, patch), F32),
            pltpu.VMEM((patch, patch), F32),
            pltpu.VMEM((n_outer, layer_rows, patch), F32),
            pltpu.VMEM((n_outer, layer_rows, patch), F32),
            pltpu.VMEM((INNER, chunk, patch), F32),
            pltpu.VMEM((INNER, chunk, patch), F32),
            pltpu.VMEM((n_row, chunk, patch), F32),
            pltpu.SemaphoreType.DMA((layers, lane_tiles)),
            pltpu.SemaphoreType.DMA((layers, gets)),
            pltpu.SemaphoreType.DMA((layers, gets)),
            pltpu.SemaphoreType.DMA((layers, puts)),
            pltpu.SemaphoreType.DMA((layers, puts)),
            pltpu.SemaphoreType.DMA((layers, lane_tiles)),
            pltpu.SemaphoreType.DMA((sums,)),
            pltpu.SemaphoreType.DMA((sums,)),
        ],
        compiler_params=pltpu.CompilerParams(
            collective_id=0, has_side_effects=True, vmem_limit_bytes=60 * 1024 * 1024
        ),
    )(*operands)


def solution(mesh):
    n_ty, n_tx = mesh.shape["ty"], mesh.shape["tx"]

    def per_device(object_field, probe_wave, prop_phase, amplitude, offsets, live_slots):
        patch = probe_wave.shape[1]
        scaling = 1.0 / math.sqrt(live_slots.shape[0] * n_ty * n_tx)
        owned, shared = step_call(
            n_ty,
            n_tx,
            scaling,
            object_field,
            probe_wave,
            prop_phase,
            amplitude,
            offsets,
            live_slots,
            jnp.asarray(dft_halves(patch)),
            jnp.asarray(even_odd(patch)),
        )
        return owned, shared.reshape(probe_wave.shape)

    placed = (
        P(None, None, "ty", "tx"),
        P(),
        P(),
        P(("ty", "tx"), None, None),
        P(None, ("ty", "tx")),
        P(("ty", "tx")),
    )
    return jax.shard_map(
        per_device,
        mesh=mesh,
        in_specs=placed,
        out_specs=(P(None, None, "ty", "tx"), P()),
        check_vma=False,
    )
```

```python
import functools
import math

import jax
import jax.numpy as jnp
import ml_dtypes
import numpy as np
from jax import lax
from jax.experimental import pallas as pl
from jax.experimental.pallas import tpu as pltpu
from jax.sharding import PartitionSpec as P

F32 = jnp.float32
BF16 = jnp.bfloat16
MESH = pl.DeviceIdType.MESH
LANES = 128
INNER = 4


def halves(table):
    high = table.astype(np.float32).astype(ml_dtypes.bfloat16)
    low = (table - high.astype(np.float64)).astype(ml_dtypes.bfloat16)
    return np.stack([high, low])


def dft_halves(length):
    half = length // 2
    sample = np.arange(half)[:, None]
    tables = []
    for parity in range(2):
        freq = 2 * np.arange(half)[None, :] + parity
        angle = 2.0 * math.pi * ((sample * freq) % length) / length
        cosine = np.cos(angle) / math.sqrt(length)
        sine = np.sin(angle) / math.sqrt(length)
        full = np.block([[cosine, -sine], [sine, cosine]])
        tables.append(np.stack([halves(full), halves(full.T)]))
    return np.stack(tables)


def even_odd(length):
    order = np.concatenate([np.arange(0, length, 2), np.arange(1, length, 2)])
    chosen = np.zeros((length, length), np.float32)
    chosen[order, np.arange(length)] = 1.0
    return np.stack([chosen, chosen.T]).astype(ml_dtypes.bfloat16)


def split(value):
    high = value.astype(BF16)
    low = (value - high.astype(F32)).astype(BF16)
    return high, low


def product(left, right):
    return jnp.dot(left, right, preferred_element_type=F32)


def from_right(value, table):
    high, low = split(value)
    left = jnp.concatenate([high, low, high], axis=1)
    return product(left, jnp.concatenate([table[0], table[0], table[1]], axis=0))


def from_left(table, value):
    high, low = split(value)
    right = jnp.concatenate([high, low, high], axis=0)
    return product(jnp.concatenate([table[0], table[0], table[1]], axis=1), right)


def thirds(value):
    high = value.astype(BF16)
    rest = value - high.astype(F32)
    middle = rest.astype(BF16)
    low = (rest - middle.astype(F32)).astype(BF16)
    return high, middle, low


def reorder(value, chosen, chosen_t):
    pieces = thirds(value)
    across = sum(product(piece, chosen) for piece in pieces)
    return sum(product(chosen_t, piece) for piece in thirds(across))


def beside(left, right):
    return jnp.concatenate([left, right], axis=1)


def above(top, bottom):
    return jnp.concatenate([top, bottom], axis=0)


def forward(real, imag, tables):
    n = LANES
    even = from_right(
        beside(real[:, :n] + real[:, n:], imag[:, :n] + imag[:, n:]), tables[0, 0]
    )
    odd = from_right(
        beside(real[:, :n] - real[:, n:], imag[:, :n] - imag[:, n:]), tables[1, 0]
    )
    real = beside(even[:, :n], odd[:, :n])
    imag = beside(even[:, n:], odd[:, n:])
    even = from_left(tables[0, 1], above(real[:n] + real[n:], imag[:n] + imag[n:]))
    odd = from_left(tables[1, 1], above(real[:n] - real[n:], imag[:n] - imag[n:]))
    return above(even[:n], odd[:n]), above(even[n:], odd[n:])


def backward(real, imag, tables):
    n = LANES
    even = from_left(tables[0, 0], above(real[:n], imag[:n]))
    odd = from_left(tables[1, 0], above(real[n:], imag[n:]))
    total, change = even + odd, even - odd
    real, imag = above(total[:n], change[:n]), above(total[n:], change[n:])
    even = from_right(beside(real[:, :n], imag[:, :n]), tables[0, 1])
    odd = from_right(beside(real[:, n:], imag[:, n:]), tables[1, 1])
    total, change = even + odd, even - odd
    return beside(total[:, :n], change[:, :n]), beside(total[:, n:], change[:, n:])


def step_kernel(
    n_ty,
    n_tx,
    scaling,
    obj,
    probe,
    phase,
    amplitude,
    offsets,
    live,
    tables,
    chosen,
    grad,
    probe_grad,
    wide_first,
    wide_second,
    padded_first,
    padded_second,
    total,
    from_left_tile,
    from_above,
    psi,
    trans,
    prop,
    target,
    probe_part,
    pair_part,
    layer_part,
    outer_part,
    inner_part,
    row_part,
    local_sem,
    get_send,
    get_recv,
    put_send,
    put_recv,
    out_sem,
    sum_send,
    sum_recv,
):
    wide = (wide_first, wide_second)
    padded = (padded_first, padded_second)
    layers, _, tile, _ = obj.shape
    patch = probe.shape[1]
    slots = amplitude.shape[0]
    lane_tiles = tile // LANES
    strip_tiles = patch // LANES
    all_tiles = lane_tiles + strip_tiles
    lower = tile - patch
    ty, tx = lax.axis_index("ty"), lax.axis_index("tx")
    left = (ty, lax.rem(tx + n_tx - 1, n_tx))
    right = (ty, lax.rem(tx + 1, n_tx))
    up = (lax.rem(ty + n_ty - 1, n_ty), tx)
    down = (lax.rem(ty + 1, n_ty), tx)

    n_row, n_outer = n_ty // 2, n_tx // INNER
    core, row = lax.rem(ty, 2), lax.div(ty, 2)
    inner, outer = lax.rem(tx, INNER), lax.div(tx, INNER)
    partner = (ty + 1 - 2 * core, tx)

    def outer_peer(step):
        index = lax.rem(outer + step, n_outer)
        return index, (ty, index * INNER + inner)

    def inner_peer(step):
        index = lax.rem(inner + step, INNER)
        return index, (ty, outer * INNER + index)

    def row_peer(step):
        index = lax.rem(row + step, n_row)
        return index, (index * 2 + core, tx)

    barrier = pltpu.get_barrier_semaphore()
    greeted = [left, right, up, down, partner]
    greeted += [outer_peer(step)[1] for step in range(1, n_outer)]
    greeted += [inner_peer(step)[1] for step in range(1, INNER)]
    greeted += [row_peer(step)[1] for step in range(1, n_row)]
    for device in greeted:
        pl.semaphore_signal(barrier, inc=1, device_id=device, device_id_type=MESH)
    pl.semaphore_wait(barrier, len(greeted))

    def remote(source, destination, send, recv, device):
        return pltpu.make_async_remote_copy(
            src_ref=source,
            dst_ref=destination,
            send_sem=send,
            recv_sem=recv,
            device_id=device,
            device_id_type=MESH,
        )

    def columns(j):
        return pl.ds(j * LANES, LANES)

    def get(s, source, destination, index, device):
        return remote(source, destination, get_send.at[s, index], get_recv.at[s, index], device)

    def get_right(s, block):
        first, size = ((0, patch), (patch, lower))[block]
        return [
            get(
                s,
                obj.at[s, :, pl.ds(first, size), columns(j)],
                wide[s].at[:, lane_tiles + j, pl.ds(first, size), :],
                block * strip_tiles + j,
                left,
            )
            for j in range(strip_tiles)
        ]

    def get_below(s):
        return [
            get(
                s,
                obj.at[s, :, pl.ds(0, patch), columns(j)],
                wide[s].at[:, j, pl.ds(tile, patch), :],
                2 * strip_tiles + j,
                up,
            )
            for j in range(lane_tiles)
        ]

    def get_corner(s, j):
        return get(
            s,
            wide[s].at[:, lane_tiles + j, pl.ds(0, patch), :],
            wide[s].at[:, lane_tiles + j, pl.ds(tile, patch), :],
            2 * strip_tiles + lane_tiles + j,
            up,
        )

    def start_get(s):
        for copy in get_right(s, 0) + get_below(s) + get_right(s, 1):
            copy.start()

    def relay_get(s):
        for j, copy in enumerate(get_right(s, 0)):
            copy.wait_recv()
            get_corner(s, j).start()

    def finish_get(s):
        for copy in get_right(s, 1) + get_below(s):
            copy.wait_recv()
        for j in range(strip_tiles):
            get_corner(s, j).wait_recv()

    def sent_get(s):
        for copy in get_right(s, 0) + get_right(s, 1) + get_below(s):
            copy.wait_send()

    def sent_corner(s):
        for j in range(strip_tiles):
            get_corner(s, j).wait_send()

    def put(s, source, destination, index, device):
        return remote(source, destination, put_send.at[s, index], put_recv.at[s, index], device)

    def put_corner(s, j):
        return put(
            s,
            total.at[s, :, lane_tiles + j, pl.ds(tile, patch), :],
            from_above.at[s, :, lane_tiles + j, :, :],
            j,
            down,
        )

    def put_top(s, j):
        return put(
            s,
            total.at[s, :, lane_tiles + j, pl.ds(0, patch), :],
            from_left_tile.at[s, :, j, pl.ds(0, patch), :],
            strip_tiles + j,
            right,
        )

    def put_bottom(s):
        return put(
            s,
            total.at[s, :, pl.ds(lane_tiles, strip_tiles), pl.ds(patch, lower), :],
            from_left_tile.at[s, :, :, pl.ds(patch, lower), :],
            2 * strip_tiles,
            right,
        )

    def put_below(s):
        return put(
            s,
            total.at[s, :, pl.ds(0, lane_tiles), pl.ds(tile, patch), :],
            from_above.at[s, :, pl.ds(0, lane_tiles), :, :],
            2 * strip_tiles + 1,
            down,
        )

    def start_corners(s):
        for j in range(strip_tiles):
            put_corner(s, j).start()

    def relay_put(s, j):
        put_corner(s, j).wait_recv()

        def add_rows(block, carry):
            rows = pl.ds(pl.multiple_of(block * 64, 64), 64)
            for part in range(2):
                total[s, part, lane_tiles + j, rows, :] += from_above[
                    s, part, lane_tiles + j, rows, :
                ]
            return carry

        lax.fori_loop(0, patch // 64, add_rows, 0)
        put_top(s, j).start()

    def out_copies(s):
        return [
            pltpu.make_async_copy(
                total.at[s, :, j, pl.ds(0, tile), :],
                grad.at[s, :, :, columns(j)],
                out_sem.at[s, j],
            )
            for j in range(lane_tiles)
        ]

    def finish_put(s):
        put_bottom(s).wait_recv()
        put_below(s).wait_recv()
        for j in range(strip_tiles):
            put_top(s, j).wait_recv()

        def add_rows(block, carry):
            rows = pl.ds(pl.multiple_of(block * 64, 64), 64)
            for part in range(2):
                for j in range(strip_tiles):
                    total[s, part, j, rows, :] += from_left_tile[s, part, j, rows, :]
            return carry

        def add_above(block, carry):
            rows = pl.ds(pl.multiple_of(block * 64, 64), 64)
            for part in range(2):
                for j in range(lane_tiles):
                    total[s, part, j, rows, :] += from_above[s, part, j, rows, :]
            return carry

        lax.fori_loop(0, tile // 64, add_rows, 0)
        lax.fori_loop(0, patch // 64, add_above, 0)
        for copy in out_copies(s):
            copy.start()

    def summed(source, destination, index, device):
        return remote(source, destination, sum_send.at[index], sum_recv.at[index], device)

    first_outer = 1
    first_inner = first_outer + n_outer
    first_row = first_inner + INNER
    second_outer = first_row + n_row
    last_pair = second_outer + n_outer

    def stage(count, peer, base, mine, source, target_of):
        def sending(step):
            index, device = peer(step)
            return remote(
                source(index),
                target_of(mine),
                sum_send.at[base + index],
                sum_recv.at[base + mine],
                device,
            )

        def receiving(step):
            index, device = peer(step)
            return remote(
                source(index),
                target_of(index),
                sum_send.at[base + index],
                sum_recv.at[base + index],
                device,
            )

        def start():
            for step in range(1, count):
                sending(step).start()

        def finish():
            for step in range(1, count):
                receiving(step).wait_recv()

        def sent():
            for step in range(1, count):
                sending(step).wait_send()

        return start, finish, sent

    def pair_sum():
        return summed(probe_part.at[1 - core], pair_part, 0, partner)

    def pair_gather():
        return summed(probe_grad.at[core], probe_grad.at[core], last_pair, partner)

    def pair_arrival():
        return summed(probe_grad.at[1 - core], probe_grad.at[1 - core], last_pair, partner)

    outer_sum = stage(
        n_outer, outer_peer, first_outer, outer,
        lambda index: layer_part.at[index], lambda index: outer_part.at[index],
    )
    inner_sum = stage(
        INNER, inner_peer, first_inner, inner,
        lambda index: inner_part.at[inner], lambda index: inner_part.at[index],
    )
    row_sum = stage(
        n_row, row_peer, first_row, row,
        lambda index: row_part.at[row], lambda index: row_part.at[index],
    )
    outer_gather = stage(
        n_outer, outer_peer, second_outer, outer,
        lambda index: probe_grad.at[core, outer],
        lambda index: probe_grad.at[core, index],
    )

    def after_pair():
        pair_sum().wait_recv()
        for index in range(n_outer):
            rows = pl.ds(index * layer_part.shape[1], layer_part.shape[1])
            layer_part[index] = probe_part[core, rows, :] + pair_part[rows, :]
        outer_part[outer] = layer_part[outer]
        outer_sum[0]()

    def reduced(parts, count):
        value = parts[0]
        for index in range(1, count):
            value += parts[index]
        return value

    def after_outer():
        outer_sum[1]()
        inner_part[inner] = reduced(outer_part, n_outer)
        inner_sum[0]()

    def after_inner():
        inner_sum[1]()
        row_part[row] = reduced(inner_part, INNER)
        row_sum[0]()

    def after_row():
        row_sum[1]()
        probe_grad[core, outer] = reduced(row_part, n_row) * scaling
        outer_gather[0]()

    def after_outer_gather():
        outer_gather[1]()
        pair_gather().start()

    def finish_sum():
        pair_arrival().wait_recv()
        pair_gather().wait_send()
        pair_sum().wait_send()
        for part in (outer_sum, inner_sum, row_sum, outer_gather):
            part[2]()

    start_get(0)
    local = [
        pltpu.make_async_copy(
            obj.at[s, :, :, columns(j)], wide[s].at[:, j, pl.ds(0, tile), :], local_sem.at[s, j]
        )
        for s in range(layers)
        for j in range(lane_tiles)
    ]
    for copy in local:
        copy.start()

    def clear(q, carry):
        margin = jnp.zeros((tile, LANES), F32)
        for s in range(layers):
            for part in range(2):
                for j in range(strip_tiles + 1):
                    padded[s][q, part, j, pl.ds(0, tile), :] = margin
                    padded[s][q, part, j, pl.ds(tile + patch, tile), :] = margin
        return carry

    lax.fori_loop(0, slots, clear, 0)

    def order_target(q, carry):
        target[q] = reorder(amplitude[q], chosen[0], chosen[1])
        return carry

    lax.fori_loop(0, slots, order_target, 0)
    angle = reorder(phase[...], chosen[0], chosen[1])
    prop[0] = jnp.cos(angle)
    prop[1] = jnp.sin(angle)
    for copy in local:
        copy.wait()
    relay_get(0)
    sent_get(0)
    start_get(1)
    finish_get(0)

    lane = lax.broadcasted_iota(jnp.int32, (patch, LANES), 1)

    def place(q):
        row, column = offsets[0, q], offsets[1, q]
        return row, lax.shift_right_logical(column, 7), lax.bitwise_and(column, LANES - 1)

    def window(s, part, q):
        row, tile_index, shift = place(q)
        back = lax.bitwise_and(LANES - shift, LANES - 1)
        rolled = [
            pltpu.roll(wide[s][part, tile_index + k, pl.ds(row, patch), :], back, 1)
            for k in range(strip_tiles + 1)
        ]
        keep = lane < LANES - shift
        return jnp.concatenate(
            [jnp.where(keep, rolled[k], rolled[k + 1]) for k in range(strip_tiles)], axis=1
        )

    def deposit(s, q, part, piece):
        _, _, shift = place(q)
        rolled = [
            pltpu.roll(piece[:, k * LANES : (k + 1) * LANES], shift, 1) for k in range(strip_tiles)
        ]
        rolled = [jnp.zeros((patch, LANES), F32)] + rolled + [jnp.zeros((patch, LANES), F32)]
        keep = lane >= shift
        for k in range(strip_tiles + 1):
            padded[s][q, part, k, pl.ds(tile, patch), :] = jnp.where(keep, rolled[k + 1], rolled[k])

    def gather(s, tiles, first, size):
        places = [place(q) for q in range(slots)]
        alive = [live[q].astype(F32) for q in range(slots)]

        def rows_of(block, carry):
            begin = first + block * 64
            for j in tiles:
                weights, sources = [], []
                for q in range(slots):
                    inside = j - places[q][1]
                    valid = jnp.logical_and(inside >= 0, inside <= strip_tiles)
                    weights.append(jnp.where(valid, alive[q], 0.0))
                    sources.append(jnp.clip(inside, 0, strip_tiles))
                for part in range(2):
                    value = jnp.zeros((64, LANES), F32)
                    for q in range(slots):
                        rows = pl.ds(tile - places[q][0] + begin, 64)
                        value += weights[q] * padded[s][q, part, sources[q], rows, :]
                    total[s, part, j, pl.ds(pl.multiple_of(begin, 64), 64), :] = value
            return carry

        lax.fori_loop(0, size // 64, rows_of, 0)

    def first_layer(q, carry):
        trans_real, trans_imag = window(0, 0, q), window(0, 1, q)
        trans[q, 0], trans[q, 1] = trans_real, trans_imag
        freq_real, freq_imag = forward(
            trans_real * probe[0] - trans_imag * probe[1],
            trans_real * probe[1] + trans_imag * probe[0],
            tables,
        )
        psi[q, 0], psi[q, 1] = backward(
            prop[0] * freq_real - prop[1] * freq_imag,
            prop[0] * freq_imag + prop[1] * freq_real,
            tables,
        )
        return carry

    lax.fori_loop(0, slots, first_layer, 0)
    sent_corner(0)
    relay_get(1)
    sent_get(1)
    finish_get(1)
    sent_corner(1)

    def second_layer(q, carry):
        trans_real, trans_imag = window(1, 0, q), window(1, 1, q)
        wave_real, wave_imag = psi[q, 0], psi[q, 1]
        freq_real, freq_imag = forward(
            trans_real * wave_real - trans_imag * wave_imag,
            trans_real * wave_imag + trans_imag * wave_real,
            tables,
        )
        energy = freq_real * freq_real + freq_imag * freq_imag + 0.25
        factor = target[q] / jnp.sqrt(energy) - 1.0
        back_real, back_imag = backward(freq_real * factor, freq_imag * factor, tables)
        wave_real, wave_imag = psi[q, 0], psi[q, 1]
        deposit(1, q, 0, wave_real * back_real + wave_imag * back_imag)
        deposit(1, q, 1, wave_real * back_imag - wave_imag * back_real)
        trans_real, trans_imag = window(1, 0, q), window(1, 1, q)
        psi[q, 0] = trans_real * back_real + trans_imag * back_imag
        psi[q, 1] = trans_real * back_imag - trans_imag * back_real
        return carry

    lax.fori_loop(0, slots, second_layer, 0)
    strip = range(lane_tiles, all_tiles)
    own = range(lane_tiles)

    gather(1, strip, 0, tile + patch)
    start_corners(1)
    put_bottom(1).start()
    gather(1, own, tile, patch)
    probe_part[...] = jnp.zeros(probe_part.shape, F32)

    def third_layer(q, carry):
        freq_real, freq_imag = forward(psi[q, 0], psi[q, 1], tables)
        back_real, back_imag = backward(
            prop[0] * freq_real + prop[1] * freq_imag,
            prop[0] * freq_imag - prop[1] * freq_real,
            tables,
        )
        deposit(0, q, 0, probe[0] * back_real + probe[1] * back_imag)
        deposit(0, q, 1, probe[0] * back_imag - probe[1] * back_real)
        weight = live[q].astype(F32)
        probe_part[0] += weight * (trans[q, 0] * back_real + trans[q, 1] * back_imag)
        probe_part[1] += weight * (trans[q, 0] * back_imag - trans[q, 1] * back_real)
        return carry

    lax.fori_loop(0, slots, third_layer, 0)
    pair_sum().start()
    for j in range(strip_tiles):
        relay_put(1, j)
    after_pair()
    put_below(1).start()
    gather(0, strip, 0, tile + patch)
    start_corners(0)
    gather(0, own, tile, patch)
    gather(1, own, 0, tile)
    after_outer()
    put_bottom(0).start()
    gather(0, own, 0, tile)
    after_inner()
    relay_put(0, 0)
    after_row()
    relay_put(0, 1)
    put_below(0).start()
    finish_put(1)
    after_outer_gather()
    finish_put(0)
    finish_sum()
    for s in range(layers):
        put_bottom(s).wait_send()
        put_below(s).wait_send()
        for j in range(strip_tiles):
            put_corner(s, j).wait_send()
            put_top(s, j).wait_send()
        for copy in out_copies(s):
            copy.wait()


def step_call(n_ty, n_tx, scaling, *operands):
    obj, probe, _, amplitude, _, _, _, _ = operands
    layers, _, tile, _ = obj.shape
    patch = probe.shape[1]
    slots = amplitude.shape[0]
    lane_tiles, strip_tiles = tile // LANES, patch // LANES
    all_tiles = lane_tiles + strip_tiles
    gets = 3 * strip_tiles + lane_tiles
    puts = 2 * strip_tiles + 2
    n_row, n_outer = n_ty // 2, n_tx // INNER
    layer_rows = patch // n_outer
    sums = 2 * n_outer + INNER + n_row + 2
    vmem = pl.BlockSpec(memory_space=pltpu.VMEM)
    smem = pl.BlockSpec(memory_space=pltpu.SMEM)
    whole = pl.BlockSpec(memory_space=pl.ANY)
    return pl.pallas_call(
        functools.partial(step_kernel, n_ty, n_tx, scaling),
        name="step",
        out_shape=(
            jax.ShapeDtypeStruct(obj.shape, F32),
            jax.ShapeDtypeStruct((2, n_outer, layer_rows, patch), F32),
        ),
        in_specs=[whole, vmem, vmem, vmem, smem, smem, vmem, vmem],
        out_specs=(whole, vmem),
        scratch_shapes=[
            pltpu.VMEM((2, all_tiles, tile + patch, LANES), F32),
            pltpu.VMEM((2, all_tiles, tile + patch, LANES), F32),
            pltpu.VMEM((slots, 2, strip_tiles + 1, 2 * tile + patch, LANES), F32),
            pltpu.VMEM((slots, 2, strip_tiles + 1, 2 * tile + patch, LANES), F32),
            pltpu.VMEM((layers, 2, all_tiles, tile + patch, LANES), F32),
            pltpu.VMEM((layers, 2, strip_tiles, tile, LANES), F32),
            pltpu.VMEM((layers, 2, all_tiles, patch, LANES), F32),
            pltpu.VMEM((slots, 2, patch, patch), F32),
            pltpu.VMEM((slots, 2, patch, patch), F32),
            pltpu.VMEM((2, patch, patch), F32),
            pltpu.VMEM((slots, patch, patch), F32),
            pltpu.VMEM((2, patch, patch), F32),
            pltpu.VMEM((patch, patch), F32),
            pltpu.VMEM((n_outer, layer_rows, patch), F32),
            pltpu.VMEM((n_outer, layer_rows, patch), F32),
            pltpu.VMEM((INNER, layer_rows, patch), F32),
            pltpu.VMEM((n_row, layer_rows, patch), F32),
            pltpu.SemaphoreType.DMA((layers, lane_tiles)),
            pltpu.SemaphoreType.DMA((layers, gets)),
            pltpu.SemaphoreType.DMA((layers, gets)),
            pltpu.SemaphoreType.DMA((layers, puts)),
            pltpu.SemaphoreType.DMA((layers, puts)),
            pltpu.SemaphoreType.DMA((layers, lane_tiles)),
            pltpu.SemaphoreType.DMA((sums,)),
            pltpu.SemaphoreType.DMA((sums,)),
        ],
        compiler_params=pltpu.CompilerParams(
            collective_id=0, has_side_effects=True, vmem_limit_bytes=60 * 1024 * 1024
        ),
    )(*operands)


def solution(mesh):
    n_ty, n_tx = mesh.shape["ty"], mesh.shape["tx"]

    def per_device(object_field, probe_wave, prop_phase, amplitude, offsets, live_slots):
        patch = probe_wave.shape[1]
        scaling = 1.0 / math.sqrt(live_slots.shape[0] * n_ty * n_tx)
        owned, shared = step_call(
            n_ty,
            n_tx,
            scaling,
            object_field,
            probe_wave,
            prop_phase,
            amplitude,
            offsets,
            live_slots,
            jnp.asarray(dft_halves(patch)),
            jnp.asarray(even_odd(patch)),
        )
        return owned, shared.reshape(probe_wave.shape)

    placed = (
        P(None, None, "ty", "tx"),
        P(),
        P(),
        P(("ty", "tx"), None, None),
        P(None, ("ty", "tx")),
        P(("ty", "tx")),
    )
    return jax.shard_map(
        per_device,
        mesh=mesh,
        in_specs=placed,
        out_specs=(P(None, None, "ty", "tx"), P()),
        check_vma=False,
    )
```

```python
import functools
import math

import jax
import jax.numpy as jnp
import ml_dtypes
import numpy as np
from jax import lax
from jax.experimental import pallas as pl
from jax.experimental.pallas import tpu as pltpu
from jax.sharding import PartitionSpec as P

F32 = jnp.float32
BF16 = jnp.bfloat16
MESH = pl.DeviceIdType.MESH
LANES = 128
INNER = 4


def halves(table):
    high = table.astype(np.float32).astype(ml_dtypes.bfloat16)
    low = (table - high.astype(np.float64)).astype(ml_dtypes.bfloat16)
    return np.stack([high, low])


def dft_halves(length):
    half = length // 2
    sample = np.arange(half)[:, None]
    tables = []
    for parity in range(2):
        freq = 2 * np.arange(half)[None, :] + parity
        angle = 2.0 * math.pi * ((sample * freq) % length) / length
        cosine = np.cos(angle) / math.sqrt(length)
        sine = np.sin(angle) / math.sqrt(length)
        full = np.block([[cosine, -sine], [sine, cosine]])
        tables.append(np.stack([halves(full), halves(full.T)]))
    return np.stack(tables)


def even_odd(length):
    order = np.concatenate([np.arange(0, length, 2), np.arange(1, length, 2)])
    chosen = np.zeros((length, length), np.float32)
    chosen[order, np.arange(length)] = 1.0
    return np.stack([chosen, chosen.T]).astype(ml_dtypes.bfloat16)


def split(value):
    high = value.astype(BF16)
    low = (value - high.astype(F32)).astype(BF16)
    return high, low


def product(left, right):
    return jnp.dot(left, right, preferred_element_type=F32)


def from_right(value, table):
    high, low = split(value)
    left = jnp.concatenate([high, low, high], axis=1)
    return product(left, jnp.concatenate([table[0], table[0], table[1]], axis=0))


def from_left(table, value):
    high, low = split(value)
    right = jnp.concatenate([high, low, high], axis=0)
    return product(jnp.concatenate([table[0], table[0], table[1]], axis=1), right)


def thirds(value):
    high = value.astype(BF16)
    rest = value - high.astype(F32)
    middle = rest.astype(BF16)
    low = (rest - middle.astype(F32)).astype(BF16)
    return high, middle, low


def reorder(value, chosen, chosen_t):
    pieces = thirds(value)
    across = sum(product(piece, chosen) for piece in pieces)
    return sum(product(chosen_t, piece) for piece in thirds(across))


def beside(left, right):
    return jnp.concatenate([left, right], axis=1)


def above(top, bottom):
    return jnp.concatenate([top, bottom], axis=0)


def forward(real, imag, tables):
    n = LANES
    even = from_right(
        beside(real[:, :n] + real[:, n:], imag[:, :n] + imag[:, n:]), tables[0, 0]
    )
    odd = from_right(
        beside(real[:, :n] - real[:, n:], imag[:, :n] - imag[:, n:]), tables[1, 0]
    )
    real = beside(even[:, :n], odd[:, :n])
    imag = beside(even[:, n:], odd[:, n:])
    even = from_left(tables[0, 1], above(real[:n] + real[n:], imag[:n] + imag[n:]))
    odd = from_left(tables[1, 1], above(real[:n] - real[n:], imag[:n] - imag[n:]))
    return above(even[:n], odd[:n]), above(even[n:], odd[n:])


def backward(real, imag, tables):
    n = LANES
    even = from_left(tables[0, 0], above(real[:n], imag[:n]))
    odd = from_left(tables[1, 0], above(real[n:], imag[n:]))
    total, change = even + odd, even - odd
    real, imag = above(total[:n], change[:n]), above(total[n:], change[n:])
    even = from_right(beside(real[:, :n], imag[:, :n]), tables[0, 1])
    odd = from_right(beside(real[:, n:], imag[:, n:]), tables[1, 1])
    total, change = even + odd, even - odd
    return beside(total[:, :n], change[:, :n]), beside(total[:, n:], change[:, n:])


def step_kernel(
    n_ty,
    n_tx,
    scaling,
    obj,
    probe,
    phase,
    amplitude,
    offsets,
    live,
    tables,
    chosen,
    grad,
    probe_grad,
    wide_first,
    wide_second,
    padded_first,
    padded_second,
    total,
    from_left_tile,
    from_above,
    psi,
    trans,
    prop,
    target,
    probe_part,
    pair_part,
    pair_sums,
    row_part,
    row_sums,
    outer_part,
    inner_part,
    local_sem,
    get_send,
    get_recv,
    put_send,
    put_recv,
    out_sem,
    sum_send,
    sum_recv,
):
    wide = (wide_first, wide_second)
    padded = (padded_first, padded_second)
    layers, _, tile, _ = obj.shape
    patch = probe.shape[1]
    slots = amplitude.shape[0]
    lane_tiles = tile // LANES
    strip_tiles = patch // LANES
    all_tiles = lane_tiles + strip_tiles
    lower = tile - patch
    ty, tx = lax.axis_index("ty"), lax.axis_index("tx")
    left = (ty, lax.rem(tx + n_tx - 1, n_tx))
    right = (ty, lax.rem(tx + 1, n_tx))
    up = (lax.rem(ty + n_ty - 1, n_ty), tx)
    down = (lax.rem(ty + 1, n_ty), tx)

    n_row, n_outer = n_ty // 2, n_tx // INNER
    core, row = lax.rem(ty, 2), lax.div(ty, 2)
    inner, outer = lax.rem(tx, INNER), lax.div(tx, INNER)
    partner = (ty + 1 - 2 * core, tx)

    def outer_peer(step):
        index = lax.rem(outer + step, n_outer)
        return index, (ty, index * INNER + inner)

    def inner_peer(step):
        index = lax.rem(inner + step, INNER)
        return index, (ty, outer * INNER + index)

    def row_peer(step):
        index = lax.rem(row + step, n_row)
        return index, (index * 2 + core, tx)

    barrier = pltpu.get_barrier_semaphore()
    greeted = [left, right, up, down, partner]
    greeted += [outer_peer(step)[1] for step in range(1, n_outer)]
    greeted += [inner_peer(step)[1] for step in range(1, INNER)]
    greeted += [row_peer(step)[1] for step in range(1, n_row)]
    for device in greeted:
        pl.semaphore_signal(barrier, inc=1, device_id=device, device_id_type=MESH)
    pl.semaphore_wait(barrier, len(greeted))

    def remote(source, destination, send, recv, device):
        return pltpu.make_async_remote_copy(
            src_ref=source,
            dst_ref=destination,
            send_sem=send,
            recv_sem=recv,
            device_id=device,
            device_id_type=MESH,
        )

    def columns(j):
        return pl.ds(j * LANES, LANES)

    def get(s, source, destination, index, device):
        return remote(source, destination, get_send.at[s, index], get_recv.at[s, index], device)

    def get_right(s, block):
        first, size = ((0, patch), (patch, lower))[block]
        return [
            get(
                s,
                obj.at[s, :, pl.ds(first, size), columns(j)],
                wide[s].at[:, lane_tiles + j, pl.ds(first, size), :],
                block * strip_tiles + j,
                left,
            )
            for j in range(strip_tiles)
        ]

    def get_below(s):
        return [
            get(
                s,
                obj.at[s, :, pl.ds(0, patch), columns(j)],
                wide[s].at[:, j, pl.ds(tile, patch), :],
                2 * strip_tiles + j,
                up,
            )
            for j in range(lane_tiles)
        ]

    def get_corner(s, j):
        return get(
            s,
            wide[s].at[:, lane_tiles + j, pl.ds(0, patch), :],
            wide[s].at[:, lane_tiles + j, pl.ds(tile, patch), :],
            2 * strip_tiles + lane_tiles + j,
            up,
        )

    def start_get(s):
        for copy in get_right(s, 0) + get_below(s) + get_right(s, 1):
            copy.start()

    def relay_get(s):
        for j, copy in enumerate(get_right(s, 0)):
            copy.wait_recv()
            get_corner(s, j).start()

    def finish_get(s):
        for copy in get_right(s, 1) + get_below(s):
            copy.wait_recv()
        for j in range(strip_tiles):
            get_corner(s, j).wait_recv()

    def sent_get(s):
        for copy in get_right(s, 0) + get_right(s, 1) + get_below(s):
            copy.wait_send()

    def sent_corner(s):
        for j in range(strip_tiles):
            get_corner(s, j).wait_send()

    def put(s, source, destination, index, device):
        return remote(source, destination, put_send.at[s, index], put_recv.at[s, index], device)

    def put_corner(s, j):
        return put(
            s,
            total.at[s, :, lane_tiles + j, pl.ds(tile, patch), :],
            from_above.at[s, :, lane_tiles + j, :, :],
            j,
            down,
        )

    def put_top(s, j):
        return put(
            s,
            total.at[s, :, lane_tiles + j, pl.ds(0, patch), :],
            from_left_tile.at[s, :, j, pl.ds(0, patch), :],
            strip_tiles + j,
            right,
        )

    def put_bottom(s):
        return put(
            s,
            total.at[s, :, pl.ds(lane_tiles, strip_tiles), pl.ds(patch, lower), :],
            from_left_tile.at[s, :, :, pl.ds(patch, lower), :],
            2 * strip_tiles,
            right,
        )

    def put_below(s):
        return put(
            s,
            total.at[s, :, pl.ds(0, lane_tiles), pl.ds(tile, patch), :],
            from_above.at[s, :, pl.ds(0, lane_tiles), :, :],
            2 * strip_tiles + 1,
            down,
        )

    def start_corners(s):
        for j in range(strip_tiles):
            put_corner(s, j).start()

    def add_corner(s, j):
        put_corner(s, j).wait_recv()

        def add_rows(block, carry):
            rows = pl.ds(pl.multiple_of(block * 64, 64), 64)
            for part in range(2):
                total[s, part, lane_tiles + j, rows, :] += from_above[
                    s, part, lane_tiles + j, rows, :
                ]
            return carry

        lax.fori_loop(0, patch // 64, add_rows, 0)

    def out_copies(s):
        return [
            pltpu.make_async_copy(
                total.at[s, :, j, pl.ds(0, tile), :],
                grad.at[s, :, :, columns(j)],
                out_sem.at[s, j],
            )
            for j in range(lane_tiles)
        ]

    def finish_put(s):
        put_bottom(s).wait_recv()
        put_below(s).wait_recv()
        for j in range(strip_tiles):
            put_top(s, j).wait_recv()

        def add_rows(block, carry):
            rows = pl.ds(pl.multiple_of(block * 64, 64), 64)
            for part in range(2):
                for j in range(strip_tiles):
                    total[s, part, j, rows, :] += from_left_tile[s, part, j, rows, :]
            return carry

        def add_above(block, carry):
            rows = pl.ds(pl.multiple_of(block * 64, 64), 64)
            for part in range(2):
                for j in range(lane_tiles):
                    total[s, part, j, rows, :] += from_above[s, part, j, rows, :]
            return carry

        lax.fori_loop(0, tile // 64, add_rows, 0)
        lax.fori_loop(0, patch // 64, add_above, 0)
        for copy in out_copies(s):
            copy.start()

    def summed(source, destination, index, device):
        return remote(source, destination, sum_send.at[index], sum_recv.at[index], device)

    first_row = 1
    first_outer = first_row + n_row
    first_inner = first_outer + n_outer
    second_outer = first_inner + INNER
    second_row = second_outer + n_outer
    last_pair = second_row + n_row

    def stage(count, peer, base, mine, source, target_of):
        def sending(step):
            index, device = peer(step)
            return remote(
                source(index),
                target_of(mine),
                sum_send.at[base + index],
                sum_recv.at[base + mine],
                device,
            )

        def receiving(step):
            index, device = peer(step)
            return remote(
                source(index),
                target_of(index),
                sum_send.at[base + index],
                sum_recv.at[base + index],
                device,
            )

        def start():
            for step in range(1, count):
                sending(step).start()

        def finish():
            for step in range(1, count):
                receiving(step).wait_recv()

        def sent():
            for step in range(1, count):
                sending(step).wait_send()

        return start, finish, sent

    def pair_sum():
        return summed(probe_part.at[1 - core], pair_part, 0, partner)

    def pair_gather():
        return summed(probe_grad.at[core], probe_grad.at[core], last_pair, partner)

    def pair_arrival():
        return summed(probe_grad.at[1 - core], probe_grad.at[1 - core], last_pair, partner)

    row_sum = stage(
        n_row, row_peer, first_row, row,
        lambda index: pair_sums.at[index], lambda index: row_part.at[index],
    )
    outer_sum = stage(
        n_outer, outer_peer, first_outer, outer,
        lambda index: row_sums.at[index], lambda index: outer_part.at[index],
    )
    inner_sum = stage(
        INNER, inner_peer, first_inner, inner,
        lambda index: inner_part.at[inner], lambda index: inner_part.at[index],
    )
    outer_gather = stage(
        n_outer, outer_peer, second_outer, outer,
        lambda index: probe_grad.at[core, row, outer],
        lambda index: probe_grad.at[core, row, index],
    )
    row_gather = stage(
        n_row, row_peer, second_row, row,
        lambda index: probe_grad.at[core, row],
        lambda index: probe_grad.at[core, index],
    )

    def reduced(parts, count):
        value = parts[0]
        for index in range(1, count):
            value += parts[index]
        return value

    def after_pair():
        pair_sum().wait_recv()
        size = pair_sums.shape[1]
        for index in range(n_row):
            rows = pl.ds(index * size, size)
            pair_sums[index] = probe_part[core, rows, :] + pair_part[rows, :]
        row_part[row] = pair_sums[row]
        row_sum[0]()

    def after_row():
        row_sum[1]()
        size = row_sums.shape[1]
        for index in range(n_outer):
            rows = pl.ds(index * size, size)
            value = row_part[0, rows, :]
            for other in range(1, n_row):
                value += row_part[other, rows, :]
            row_sums[index] = value
        outer_part[outer] = row_sums[outer]
        outer_sum[0]()

    def after_outer():
        outer_sum[1]()
        inner_part[inner] = reduced(outer_part, n_outer)
        inner_sum[0]()

    def after_inner():
        inner_sum[1]()
        probe_grad[core, row, outer] = reduced(inner_part, INNER) * scaling
        outer_gather[0]()

    def after_outer_gather():
        outer_gather[1]()
        row_gather[0]()

    def after_row_gather():
        row_gather[1]()
        pair_gather().start()

    def finish_sum():
        pair_arrival().wait_recv()
        pair_gather().wait_send()
        pair_sum().wait_send()
        for part in (row_sum, outer_sum, inner_sum, outer_gather, row_gather):
            part[2]()

    start_get(0)
    local = [
        pltpu.make_async_copy(
            obj.at[s, :, :, columns(j)], wide[s].at[:, j, pl.ds(0, tile), :], local_sem.at[s, j]
        )
        for s in range(layers)
        for j in range(lane_tiles)
    ]
    for copy in local:
        copy.start()

    def clear(q, carry):
        margin = jnp.zeros((tile, LANES), F32)
        for s in range(layers):
            for part in range(2):
                for j in range(strip_tiles + 1):
                    padded[s][q, part, j, pl.ds(0, tile), :] = margin
                    padded[s][q, part, j, pl.ds(tile + patch, tile), :] = margin
        return carry

    lax.fori_loop(0, slots, clear, 0)

    def order_target(q, carry):
        target[q] = reorder(amplitude[q], chosen[0], chosen[1])
        return carry

    lax.fori_loop(0, slots, order_target, 0)
    angle = reorder(phase[...], chosen[0], chosen[1])
    prop[0] = jnp.cos(angle)
    prop[1] = jnp.sin(angle)
    for copy in local:
        copy.wait()
    relay_get(0)
    sent_get(0)
    start_get(1)
    finish_get(0)

    lane = lax.broadcasted_iota(jnp.int32, (patch, LANES), 1)

    def place(q):
        row, column = offsets[0, q], offsets[1, q]
        return row, lax.shift_right_logical(column, 7), lax.bitwise_and(column, LANES - 1)

    def window(s, part, q):
        row, tile_index, shift = place(q)
        back = lax.bitwise_and(LANES - shift, LANES - 1)
        rolled = [
            pltpu.roll(wide[s][part, tile_index + k, pl.ds(row, patch), :], back, 1)
            for k in range(strip_tiles + 1)
        ]
        keep = lane < LANES - shift
        return jnp.concatenate(
            [jnp.where(keep, rolled[k], rolled[k + 1]) for k in range(strip_tiles)], axis=1
        )

    def deposit(s, q, part, piece):
        _, _, shift = place(q)
        rolled = [
            pltpu.roll(piece[:, k * LANES : (k + 1) * LANES], shift, 1) for k in range(strip_tiles)
        ]
        rolled = [jnp.zeros((patch, LANES), F32)] + rolled + [jnp.zeros((patch, LANES), F32)]
        keep = lane >= shift
        for k in range(strip_tiles + 1):
            padded[s][q, part, k, pl.ds(tile, patch), :] = jnp.where(keep, rolled[k + 1], rolled[k])

    def gather(s, tiles, first, size):
        places = [place(q) for q in range(slots)]
        alive = [live[q].astype(F32) for q in range(slots)]

        def rows_of(block, carry):
            begin = first + block * 64
            for j in tiles:
                weights, sources = [], []
                for q in range(slots):
                    inside = j - places[q][1]
                    valid = jnp.logical_and(inside >= 0, inside <= strip_tiles)
                    weights.append(jnp.where(valid, alive[q], 0.0))
                    sources.append(jnp.clip(inside, 0, strip_tiles))
                for part in range(2):
                    value = jnp.zeros((64, LANES), F32)
                    for q in range(slots):
                        rows = pl.ds(tile - places[q][0] + begin, 64)
                        value += weights[q] * padded[s][q, part, sources[q], rows, :]
                    total[s, part, j, pl.ds(pl.multiple_of(begin, 64), 64), :] = value
            return carry

        lax.fori_loop(0, size // 64, rows_of, 0)

    def first_layer(q, carry):
        trans_real, trans_imag = window(0, 0, q), window(0, 1, q)
        trans[q, 0], trans[q, 1] = trans_real, trans_imag
        freq_real, freq_imag = forward(
            trans_real * probe[0] - trans_imag * probe[1],
            trans_real * probe[1] + trans_imag * probe[0],
            tables,
        )
        psi[q, 0], psi[q, 1] = backward(
            prop[0] * freq_real - prop[1] * freq_imag,
            prop[0] * freq_imag + prop[1] * freq_real,
            tables,
        )
        return carry

    lax.fori_loop(0, slots, first_layer, 0)
    sent_corner(0)
    relay_get(1)
    sent_get(1)
    finish_get(1)
    sent_corner(1)

    def second_layer(q, carry):
        trans_real, trans_imag = window(1, 0, q), window(1, 1, q)
        wave_real, wave_imag = psi[q, 0], psi[q, 1]
        freq_real, freq_imag = forward(
            trans_real * wave_real - trans_imag * wave_imag,
            trans_real * wave_imag + trans_imag * wave_real,
            tables,
        )
        energy = freq_real * freq_real + freq_imag * freq_imag + 0.25
        factor = target[q] / jnp.sqrt(energy) - 1.0
        back_real, back_imag = backward(freq_real * factor, freq_imag * factor, tables)
        wave_real, wave_imag = psi[q, 0], psi[q, 1]
        deposit(1, q, 0, wave_real * back_real + wave_imag * back_imag)
        deposit(1, q, 1, wave_real * back_imag - wave_imag * back_real)
        trans_real, trans_imag = window(1, 0, q), window(1, 1, q)
        psi[q, 0] = trans_real * back_real + trans_imag * back_imag
        psi[q, 1] = trans_real * back_imag - trans_imag * back_real
        return carry

    for q in range(slots):
        second_layer(q, 0)
    strip = range(lane_tiles, all_tiles)
    own = range(lane_tiles)

    gather(1, strip, 0, tile + patch)
    start_corners(1)
    put_bottom(1).start()
    gather(1, own, tile, patch)
    probe_part[...] = jnp.zeros(probe_part.shape, F32)

    def third_layer(q, carry):
        freq_real, freq_imag = forward(psi[q, 0], psi[q, 1], tables)
        back_real, back_imag = backward(
            prop[0] * freq_real + prop[1] * freq_imag,
            prop[0] * freq_imag - prop[1] * freq_real,
            tables,
        )
        deposit(0, q, 0, probe[0] * back_real + probe[1] * back_imag)
        deposit(0, q, 1, probe[0] * back_imag - probe[1] * back_real)
        weight = live[q].astype(F32)
        probe_part[0] += weight * (trans[q, 0] * back_real + trans[q, 1] * back_imag)
        probe_part[1] += weight * (trans[q, 0] * back_imag - trans[q, 1] * back_real)
        return carry

    for q in range(slots):
        third_layer(q, 0)
    pair_sum().start()
    for j in range(strip_tiles):
        add_corner(1, j)
    after_pair()
    put_top(1, 0).start()
    gather(0, strip, 0, tile + patch)
    start_corners(0)
    put_below(1).start()
    gather(0, own, tile, patch)
    gather(1, own, 0, tile)
    after_row()
    put_top(1, 1).start()
    gather(0, own, 0, tile)
    after_outer()
    put_bottom(0).start()
    add_corner(0, 0)
    after_inner()
    put_top(0, 0).start()
    add_corner(0, 1)
    after_outer_gather()
    put_top(0, 1).start()
    put_below(0).start()
    finish_put(1)
    after_row_gather()
    finish_put(0)
    finish_sum()
    for s in range(layers):
        put_bottom(s).wait_send()
        put_below(s).wait_send()
        for j in range(strip_tiles):
            put_corner(s, j).wait_send()
            put_top(s, j).wait_send()
        for copy in out_copies(s):
            copy.wait()


def step_call(n_ty, n_tx, scaling, *operands):
    obj, probe, _, amplitude, _, _, _, _ = operands
    layers, _, tile, _ = obj.shape
    patch = probe.shape[1]
    slots = amplitude.shape[0]
    lane_tiles, strip_tiles = tile // LANES, patch // LANES
    all_tiles = lane_tiles + strip_tiles
    gets = 3 * strip_tiles + lane_tiles
    puts = 2 * strip_tiles + 2
    n_row, n_outer = n_ty // 2, n_tx // INNER
    row_rows = patch // n_row
    chunk = row_rows // n_outer
    sums = 2 * n_row + 2 * n_outer + INNER + 2
    vmem = pl.BlockSpec(memory_space=pltpu.VMEM)
    smem = pl.BlockSpec(memory_space=pltpu.SMEM)
    whole = pl.BlockSpec(memory_space=pl.ANY)
    return pl.pallas_call(
        functools.partial(step_kernel, n_ty, n_tx, scaling),
        name="step",
        out_shape=(
            jax.ShapeDtypeStruct(obj.shape, F32),
            jax.ShapeDtypeStruct((2, n_row, n_outer, chunk, patch), F32),
        ),
        in_specs=[whole, vmem, vmem, vmem, smem, smem, vmem, vmem],
        out_specs=(whole, vmem),
        scratch_shapes=[
            pltpu.VMEM((2, all_tiles, tile + patch, LANES), F32),
            pltpu.VMEM((2, all_tiles, tile + patch, LANES), F32),
            pltpu.VMEM((slots, 2, strip_tiles + 1, 2 * tile + patch, LANES), F32),
            pltpu.VMEM((slots, 2, strip_tiles + 1, 2 * tile + patch, LANES), F32),
            pltpu.VMEM((layers, 2, all_tiles, tile + patch, LANES), F32),
            pltpu.VMEM((layers, 2, strip_tiles, tile, LANES), F32),
            pltpu.VMEM((layers, 2, all_tiles, patch, LANES), F32),
            pltpu.VMEM((slots, 2, patch, patch), F32),
            pltpu.VMEM((slots, 2, patch, patch), F32),
            pltpu.VMEM((2, patch, patch), F32),
            pltpu.VMEM((slots, patch, patch), F32),
            pltpu.VMEM((2, patch, patch), F32),
            pltpu.VMEM((patch, patch), F32),
            pltpu.VMEM((n_row, row_rows, patch), F32),
            pltpu.VMEM((n_row, row_rows, patch), F32),
            pltpu.VMEM((n_outer, chunk, patch), F32),
            pltpu.VMEM((n_outer, chunk, patch), F32),
            pltpu.VMEM((INNER, chunk, patch), F32),
            pltpu.SemaphoreType.DMA((layers, lane_tiles)),
            pltpu.SemaphoreType.DMA((layers, gets)),
            pltpu.SemaphoreType.DMA((layers, gets)),
            pltpu.SemaphoreType.DMA((layers, puts)),
            pltpu.SemaphoreType.DMA((layers, puts)),
            pltpu.SemaphoreType.DMA((layers, lane_tiles)),
            pltpu.SemaphoreType.DMA((sums,)),
            pltpu.SemaphoreType.DMA((sums,)),
        ],
        compiler_params=pltpu.CompilerParams(
            collective_id=0, has_side_effects=True, vmem_limit_bytes=60 * 1024 * 1024
        ),
    )(*operands)


def solution(mesh):
    n_ty, n_tx = mesh.shape["ty"], mesh.shape["tx"]

    def per_device(object_field, probe_wave, prop_phase, amplitude, offsets, live_slots):
        patch = probe_wave.shape[1]
        scaling = 1.0 / math.sqrt(live_slots.shape[0] * n_ty * n_tx)
        owned, shared = step_call(
            n_ty,
            n_tx,
            scaling,
            object_field,
            probe_wave,
            prop_phase,
            amplitude,
            offsets,
            live_slots,
            jnp.asarray(dft_halves(patch)),
            jnp.asarray(even_odd(patch)),
        )
        return owned, shared.reshape(probe_wave.shape)

    placed = (
        P(None, None, "ty", "tx"),
        P(),
        P(),
        P(("ty", "tx"), None, None),
        P(None, ("ty", "tx")),
        P(("ty", "tx")),
    )
    return jax.shard_map(
        per_device,
        mesh=mesh,
        in_specs=placed,
        out_specs=(P(None, None, "ty", "tx"), P()),
        check_vma=False,
    )
```

```python
import functools
import math

import jax
import jax.numpy as jnp
import ml_dtypes
import numpy as np
from jax import lax
from jax.experimental import pallas as pl
from jax.experimental.pallas import tpu as pltpu
from jax.sharding import PartitionSpec as P

F32 = jnp.float32
BF16 = jnp.bfloat16
MESH = pl.DeviceIdType.MESH
LANES = 128
INNER = 4


def halves(table):
    high = table.astype(np.float32).astype(ml_dtypes.bfloat16)
    low = (table - high.astype(np.float64)).astype(ml_dtypes.bfloat16)
    return np.stack([high, low])


def dft_halves(length):
    half = length // 2
    sample = np.arange(half)[:, None]
    tables = []
    for parity in range(2):
        freq = 2 * np.arange(half)[None, :] + parity
        angle = 2.0 * math.pi * ((sample * freq) % length) / length
        cosine = np.cos(angle) / math.sqrt(length)
        sine = np.sin(angle) / math.sqrt(length)
        full = np.block([[cosine, -sine], [sine, cosine]])
        tables.append(np.stack([halves(full), halves(full.T)]))
    return np.stack(tables)


def even_odd(length):
    order = np.concatenate([np.arange(0, length, 2), np.arange(1, length, 2)])
    chosen = np.zeros((length, length), np.float32)
    chosen[order, np.arange(length)] = 1.0
    return np.stack([chosen, chosen.T]).astype(ml_dtypes.bfloat16)


def split(value):
    high = value.astype(BF16)
    low = (value - high.astype(F32)).astype(BF16)
    return high, low


def product(left, right):
    return jnp.dot(left, right, preferred_element_type=F32)


def from_right(value, table):
    high, low = split(value)
    left = jnp.concatenate([high, low, high], axis=1)
    return product(left, jnp.concatenate([table[0], table[0], table[1]], axis=0))


def from_left(table, value):
    high, low = split(value)
    right = jnp.concatenate([high, low, high], axis=0)
    return product(jnp.concatenate([table[0], table[0], table[1]], axis=1), right)


def thirds(value):
    high = value.astype(BF16)
    rest = value - high.astype(F32)
    middle = rest.astype(BF16)
    low = (rest - middle.astype(F32)).astype(BF16)
    return high, middle, low


def reorder(value, chosen, chosen_t):
    pieces = thirds(value)
    across = sum(product(piece, chosen) for piece in pieces)
    return sum(product(chosen_t, piece) for piece in thirds(across))


def beside(left, right):
    return jnp.concatenate([left, right], axis=1)


def above(top, bottom):
    return jnp.concatenate([top, bottom], axis=0)


def forward(real, imag, tables):
    n = LANES
    even = from_right(
        beside(real[:, :n] + real[:, n:], imag[:, :n] + imag[:, n:]), tables[0, 0]
    )
    odd = from_right(
        beside(real[:, :n] - real[:, n:], imag[:, :n] - imag[:, n:]), tables[1, 0]
    )
    real = beside(even[:, :n], odd[:, :n])
    imag = beside(even[:, n:], odd[:, n:])
    even = from_left(tables[0, 1], above(real[:n] + real[n:], imag[:n] + imag[n:]))
    odd = from_left(tables[1, 1], above(real[:n] - real[n:], imag[:n] - imag[n:]))
    return above(even[:n], odd[:n]), above(even[n:], odd[n:])


def backward(real, imag, tables):
    n = LANES
    even = from_left(tables[0, 0], above(real[:n], imag[:n]))
    odd = from_left(tables[1, 0], above(real[n:], imag[n:]))
    total, change = even + odd, even - odd
    real, imag = above(total[:n], change[:n]), above(total[n:], change[n:])
    even = from_right(beside(real[:, :n], imag[:, :n]), tables[0, 1])
    odd = from_right(beside(real[:, n:], imag[:, n:]), tables[1, 1])
    total, change = even + odd, even - odd
    return beside(total[:, :n], change[:, :n]), beside(total[:, n:], change[:, n:])


def step_kernel(
    n_ty,
    n_tx,
    scaling,
    obj,
    probe_given,
    phase_given,
    amplitude_given,
    offsets,
    live,
    tables_given,
    chosen_given,
    grad,
    probe_grad,
    wide_first,
    wide_second,
    padded_first,
    padded_second,
    total,
    from_left_tile,
    from_above,
    psi,
    trans,
    prop,
    target,
    probe_part,
    pair_part,
    pair_sums,
    row_part,
    row_sums,
    outer_part,
    inner_part,
    probe,
    phase,
    amplitude,
    tables,
    chosen,
    local_sem,
    given_sem,
    get_send,
    get_recv,
    put_send,
    put_recv,
    out_sem,
    sum_send,
    sum_recv,
):
    wide = (wide_first, wide_second)
    padded = (padded_first, padded_second)
    layers, _, tile, _ = obj.shape
    patch = probe.shape[1]
    slots = amplitude.shape[0]
    lane_tiles = tile // LANES
    strip_tiles = patch // LANES
    all_tiles = lane_tiles + strip_tiles
    lower = tile - patch
    ty, tx = lax.axis_index("ty"), lax.axis_index("tx")
    left = (ty, lax.rem(tx + n_tx - 1, n_tx))
    right = (ty, lax.rem(tx + 1, n_tx))
    up = (lax.rem(ty + n_ty - 1, n_ty), tx)
    down = (lax.rem(ty + 1, n_ty), tx)

    n_row, n_outer = n_ty // 2, n_tx // INNER
    core, row = lax.rem(ty, 2), lax.div(ty, 2)
    inner, outer = lax.rem(tx, INNER), lax.div(tx, INNER)
    partner = (ty + 1 - 2 * core, tx)

    def outer_peer(step):
        index = lax.rem(outer + step, n_outer)
        return index, (ty, index * INNER + inner)

    def inner_peer(step):
        index = lax.rem(inner + step, INNER)
        return index, (ty, outer * INNER + index)

    def row_peer(step):
        index = lax.rem(row + step, n_row)
        return index, (index * 2 + core, tx)

    barrier = pltpu.get_barrier_semaphore()
    greeted = [left, right, up, down, partner]
    greeted += [outer_peer(step)[1] for step in range(1, n_outer)]
    greeted += [inner_peer(step)[1] for step in range(1, INNER)]
    greeted += [row_peer(step)[1] for step in range(1, n_row)]
    for device in greeted:
        pl.semaphore_signal(barrier, inc=1, device_id=device, device_id_type=MESH)
    pl.semaphore_wait(barrier, len(greeted))

    def remote(source, destination, send, recv, device):
        return pltpu.make_async_remote_copy(
            src_ref=source,
            dst_ref=destination,
            send_sem=send,
            recv_sem=recv,
            device_id=device,
            device_id_type=MESH,
        )

    def columns(j):
        return pl.ds(j * LANES, LANES)

    def get(s, source, destination, index, device):
        return remote(source, destination, get_send.at[s, index], get_recv.at[s, index], device)

    def get_right(s, block):
        first, size = ((0, patch), (patch, lower))[block]
        return [
            get(
                s,
                obj.at[s, :, pl.ds(first, size), columns(j)],
                wide[s].at[:, lane_tiles + j, pl.ds(first, size), :],
                block * strip_tiles + j,
                left,
            )
            for j in range(strip_tiles)
        ]

    def get_below(s):
        return [
            get(
                s,
                obj.at[s, :, pl.ds(0, patch), columns(j)],
                wide[s].at[:, j, pl.ds(tile, patch), :],
                2 * strip_tiles + j,
                up,
            )
            for j in range(lane_tiles)
        ]

    def get_corner(s, j):
        return get(
            s,
            wide[s].at[:, lane_tiles + j, pl.ds(0, patch), :],
            wide[s].at[:, lane_tiles + j, pl.ds(tile, patch), :],
            2 * strip_tiles + lane_tiles + j,
            up,
        )

    def relay_get(s):
        for j, copy in enumerate(get_right(s, 0)):
            copy.wait_recv()
            get_corner(s, j).start()

    def finish_get(s):
        for copy in get_right(s, 1) + get_below(s):
            copy.wait_recv()
        for j in range(strip_tiles):
            get_corner(s, j).wait_recv()

    def sent_get(s):
        for copy in get_right(s, 0) + get_right(s, 1) + get_below(s):
            copy.wait_send()

    def sent_corner(s):
        for j in range(strip_tiles):
            get_corner(s, j).wait_send()

    def put(s, source, destination, index, device):
        return remote(source, destination, put_send.at[s, index], put_recv.at[s, index], device)

    def put_corner(s, j):
        return put(
            s,
            total.at[s, :, lane_tiles + j, pl.ds(tile, patch), :],
            from_above.at[s, :, lane_tiles + j, :, :],
            j,
            down,
        )

    def put_top(s, j):
        return put(
            s,
            total.at[s, :, lane_tiles + j, pl.ds(0, patch), :],
            from_left_tile.at[s, :, j, pl.ds(0, patch), :],
            strip_tiles + j,
            right,
        )

    def put_bottom(s):
        return put(
            s,
            total.at[s, :, pl.ds(lane_tiles, strip_tiles), pl.ds(patch, lower), :],
            from_left_tile.at[s, :, :, pl.ds(patch, lower), :],
            2 * strip_tiles,
            right,
        )

    def put_below(s):
        return put(
            s,
            total.at[s, :, pl.ds(0, lane_tiles), pl.ds(tile, patch), :],
            from_above.at[s, :, pl.ds(0, lane_tiles), :, :],
            2 * strip_tiles + 1,
            down,
        )

    def start_corners(s):
        for j in range(strip_tiles):
            put_corner(s, j).start()

    def add_corner(s, j):
        put_corner(s, j).wait_recv()

        def add_rows(block, carry):
            rows = pl.ds(pl.multiple_of(block * 64, 64), 64)
            for part in range(2):
                total[s, part, lane_tiles + j, rows, :] += from_above[
                    s, part, lane_tiles + j, rows, :
                ]
            return carry

        lax.fori_loop(0, patch // 64, add_rows, 0)

    def out_copy(s, j):
        return pltpu.make_async_copy(
            total.at[s, :, j, pl.ds(0, tile), :],
            grad.at[s, :, :, columns(j)],
            out_sem.at[s, j],
        )

    def finish_tile(s, j):
        if j < strip_tiles:
            put_top(s, j).wait_recv()

        def add_both(block, carry):
            rows = pl.ds(pl.multiple_of(block * 64, 64), 64)
            for part in range(2):
                value = total[s, part, j, rows, :] + from_above[s, part, j, rows, :]
                if j < strip_tiles:
                    value += from_left_tile[s, part, j, rows, :]
                total[s, part, j, rows, :] = value
            return carry

        def add_left(block, carry):
            rows = pl.ds(pl.multiple_of(block * 64, 64), 64)
            for part in range(2):
                total[s, part, j, rows, :] += from_left_tile[s, part, j, rows, :]
            return carry

        lax.fori_loop(0, patch // 64, add_both, 0)
        if j < strip_tiles:
            lax.fori_loop(patch // 64, tile // 64, add_left, 0)
        out_copy(s, j).start()

    def finish_put(s):
        put_bottom(s).wait_recv()
        put_below(s).wait_recv()
        for j in reversed(range(strip_tiles, lane_tiles)):
            finish_tile(s, j)
        for j in range(strip_tiles):
            finish_tile(s, j)

    def summed(source, destination, index, device):
        return remote(source, destination, sum_send.at[index], sum_recv.at[index], device)

    first_row = 1
    first_outer = first_row + n_row
    first_inner = first_outer + n_outer
    second_outer = first_inner + INNER
    second_row = second_outer + n_outer
    last_pair = second_row + n_row

    def stage(count, peer, base, mine, source, target_of):
        def sending(step):
            index, device = peer(step)
            return remote(
                source(index),
                target_of(mine),
                sum_send.at[base + index],
                sum_recv.at[base + mine],
                device,
            )

        def receiving(step):
            index, device = peer(step)
            return remote(
                source(index),
                target_of(index),
                sum_send.at[base + index],
                sum_recv.at[base + index],
                device,
            )

        def start():
            for step in range(1, count):
                sending(step).start()

        def finish():
            for step in range(1, count):
                receiving(step).wait_recv()

        def sent():
            for step in range(1, count):
                sending(step).wait_send()

        return start, finish, sent

    def pair_sum():
        return summed(probe_part.at[1 - core], pair_part, 0, partner)

    def pair_gather():
        return summed(probe_grad.at[core], probe_grad.at[core], last_pair, partner)

    def pair_arrival():
        return summed(probe_grad.at[1 - core], probe_grad.at[1 - core], last_pair, partner)

    row_sum = stage(
        n_row, row_peer, first_row, row,
        lambda index: pair_sums.at[index], lambda index: row_part.at[index],
    )
    outer_sum = stage(
        n_outer, outer_peer, first_outer, outer,
        lambda index: row_sums.at[index], lambda index: outer_part.at[index],
    )
    inner_sum = stage(
        INNER, inner_peer, first_inner, inner,
        lambda index: inner_part.at[inner], lambda index: inner_part.at[index],
    )
    outer_gather = stage(
        n_outer, outer_peer, second_outer, outer,
        lambda index: probe_grad.at[core, row, outer],
        lambda index: probe_grad.at[core, row, index],
    )
    row_gather = stage(
        n_row, row_peer, second_row, row,
        lambda index: probe_grad.at[core, row],
        lambda index: probe_grad.at[core, index],
    )

    def reduced(parts, count):
        value = parts[0]
        for index in range(1, count):
            value += parts[index]
        return value

    def after_pair():
        pair_sum().wait_recv()
        size = pair_sums.shape[1]
        for index in range(n_row):
            rows = pl.ds(index * size, size)
            pair_sums[index] = probe_part[core, rows, :] + pair_part[rows, :]
        row_part[row] = pair_sums[row]
        row_sum[0]()

    def after_row():
        row_sum[1]()
        size = row_sums.shape[1]
        for index in range(n_outer):
            rows = pl.ds(index * size, size)
            value = row_part[0, rows, :]
            for other in range(1, n_row):
                value += row_part[other, rows, :]
            row_sums[index] = value
        outer_part[outer] = row_sums[outer]
        outer_sum[0]()

    def after_outer():
        outer_sum[1]()
        inner_part[inner] = reduced(outer_part, n_outer)
        inner_sum[0]()

    def after_inner():
        inner_sum[1]()
        probe_grad[core, row, outer] = reduced(inner_part, INNER) * scaling
        outer_gather[0]()

    def after_outer_gather():
        outer_gather[1]()
        row_gather[0]()

    def after_row_gather():
        row_gather[1]()
        pair_gather().start()

    def finish_sum():
        pair_arrival().wait_recv()
        pair_gather().wait_send()
        pair_sum().wait_send()
        for part in (row_sum, outer_sum, inner_sum, outer_gather, row_gather):
            part[2]()

    for copy in get_right(0, 0) + get_below(0) + get_right(0, 1):
        copy.start()
    local = [
        pltpu.make_async_copy(
            obj.at[s, :, :, columns(j)], wide[s].at[:, j, pl.ds(0, tile), :], local_sem.at[s, j]
        )
        for s in range(layers)
        for j in range(lane_tiles)
    ]
    given = [
        pltpu.make_async_copy(source, destination, given_sem.at[index])
        for index, (source, destination) in enumerate(
            (
                (chosen_given, chosen),
                (phase_given, phase),
                (amplitude_given, amplitude),
                (probe_given, probe),
                (tables_given, tables),
            )
        )
    ]
    for copy in given + local:
        copy.start()

    def clear(q, carry):
        margin = jnp.zeros((tile, LANES), F32)
        for s in range(layers):
            for part in range(2):
                for j in range(strip_tiles + 1):
                    padded[s][q, part, j, pl.ds(0, tile), :] = margin
                    padded[s][q, part, j, pl.ds(tile + patch, tile), :] = margin
        return carry

    lax.fori_loop(0, slots, clear, 0)
    for copy in given:
        copy.wait()

    def order_target(q, carry):
        target[q] = reorder(amplitude[q], chosen[0], chosen[1])
        return carry

    lax.fori_loop(0, slots, order_target, 0)
    angle = reorder(phase[...], chosen[0], chosen[1])
    prop[0] = jnp.cos(angle)
    prop[1] = jnp.sin(angle)
    for copy in local:
        copy.wait()
    relay_get(0)
    for copy in get_right(1, 0):
        copy.start()
    finish_get(0)
    for copy in get_below(1) + get_right(1, 1):
        copy.start()
    sent_get(0)

    lane = lax.broadcasted_iota(jnp.int32, (patch, LANES), 1)

    def place(q):
        row, column = offsets[0, q], offsets[1, q]
        return row, lax.shift_right_logical(column, 7), lax.bitwise_and(column, LANES - 1)

    def window(s, part, q):
        row, tile_index, shift = place(q)
        back = lax.bitwise_and(LANES - shift, LANES - 1)
        rolled = [
            pltpu.roll(wide[s][part, tile_index + k, pl.ds(row, patch), :], back, 1)
            for k in range(strip_tiles + 1)
        ]
        keep = lane < LANES - shift
        return jnp.concatenate(
            [jnp.where(keep, rolled[k], rolled[k + 1]) for k in range(strip_tiles)], axis=1
        )

    def deposit(s, q, part, piece):
        _, _, shift = place(q)
        rolled = [
            pltpu.roll(piece[:, k * LANES : (k + 1) * LANES], shift, 1) for k in range(strip_tiles)
        ]
        rolled = [jnp.zeros((patch, LANES), F32)] + rolled + [jnp.zeros((patch, LANES), F32)]
        keep = lane >= shift
        for k in range(strip_tiles + 1):
            padded[s][q, part, k, pl.ds(tile, patch), :] = jnp.where(keep, rolled[k + 1], rolled[k])

    def gather(s, tiles, first, size):
        places = [place(q) for q in range(slots)]
        alive = [live[q].astype(F32) for q in range(slots)]

        def rows_of(block, carry):
            begin = first + block * 64
            for j in tiles:
                weights, sources = [], []
                for q in range(slots):
                    inside = j - places[q][1]
                    valid = jnp.logical_and(inside >= 0, inside <= strip_tiles)
                    weights.append(jnp.where(valid, alive[q], 0.0))
                    sources.append(jnp.clip(inside, 0, strip_tiles))
                for part in range(2):
                    value = jnp.zeros((64, LANES), F32)
                    for q in range(slots):
                        rows = pl.ds(tile - places[q][0] + begin, 64)
                        value += weights[q] * padded[s][q, part, sources[q], rows, :]
                    total[s, part, j, pl.ds(pl.multiple_of(begin, 64), 64), :] = value
            return carry

        lax.fori_loop(0, size // 64, rows_of, 0)

    def first_layer(q, carry):
        trans_real, trans_imag = window(0, 0, q), window(0, 1, q)
        trans[q, 0], trans[q, 1] = trans_real, trans_imag
        freq_real, freq_imag = forward(
            trans_real * probe[0] - trans_imag * probe[1],
            trans_real * probe[1] + trans_imag * probe[0],
            tables,
        )
        psi[q, 0], psi[q, 1] = backward(
            prop[0] * freq_real - prop[1] * freq_imag,
            prop[0] * freq_imag + prop[1] * freq_real,
            tables,
        )
        return carry

    lax.fori_loop(0, slots, first_layer, 0)
    sent_corner(0)
    relay_get(1)
    sent_get(1)
    finish_get(1)
    sent_corner(1)

    def second_layer(q, carry):
        trans_real, trans_imag = window(1, 0, q), window(1, 1, q)
        wave_real, wave_imag = psi[q, 0], psi[q, 1]
        freq_real, freq_imag = forward(
            trans_real * wave_real - trans_imag * wave_imag,
            trans_real * wave_imag + trans_imag * wave_real,
            tables,
        )
        energy = freq_real * freq_real + freq_imag * freq_imag + 0.25
        factor = target[q] / jnp.sqrt(energy) - 1.0
        back_real, back_imag = backward(freq_real * factor, freq_imag * factor, tables)
        wave_real, wave_imag = psi[q, 0], psi[q, 1]
        deposit(1, q, 0, wave_real * back_real + wave_imag * back_imag)
        deposit(1, q, 1, wave_real * back_imag - wave_imag * back_real)
        trans_real, trans_imag = window(1, 0, q), window(1, 1, q)
        psi[q, 0] = trans_real * back_real + trans_imag * back_imag
        psi[q, 1] = trans_real * back_imag - trans_imag * back_real
        return carry

    for q in range(slots):
        second_layer(q, 0)
    strip = range(lane_tiles, all_tiles)
    own = range(lane_tiles)

    gather(1, strip, 0, tile + patch)
    start_corners(1)
    put_bottom(1).start()
    gather(1, own, tile, patch)
    probe_part[...] = jnp.zeros(probe_part.shape, F32)

    def third_layer(q, carry):
        freq_real, freq_imag = forward(psi[q, 0], psi[q, 1], tables)
        back_real, back_imag = backward(
            prop[0] * freq_real + prop[1] * freq_imag,
            prop[0] * freq_imag - prop[1] * freq_real,
            tables,
        )
        deposit(0, q, 0, probe[0] * back_real + probe[1] * back_imag)
        deposit(0, q, 1, probe[0] * back_imag - probe[1] * back_real)
        weight = live[q].astype(F32)
        probe_part[0] += weight * (trans[q, 0] * back_real + trans[q, 1] * back_imag)
        probe_part[1] += weight * (trans[q, 0] * back_imag - trans[q, 1] * back_real)
        return carry

    for q in range(slots):
        third_layer(q, 0)
    pair_sum().start()
    for j in range(strip_tiles):
        add_corner(1, j)
    after_pair()
    put_top(1, 0).start()
    gather(0, strip, 0, tile + patch)
    start_corners(0)
    put_below(1).start()
    gather(0, own, tile, patch)
    gather(1, own, 0, tile)
    after_row()
    put_top(1, 1).start()
    gather(0, own, 0, tile)
    after_outer()
    put_bottom(0).start()
    add_corner(0, 0)
    after_inner()
    put_top(0, 0).start()
    add_corner(0, 1)
    after_outer_gather()
    put_top(0, 1).start()
    put_below(0).start()
    finish_put(1)
    after_row_gather()
    finish_put(0)
    finish_sum()
    for s in range(layers):
        put_bottom(s).wait_send()
        put_below(s).wait_send()
        for j in range(strip_tiles):
            put_corner(s, j).wait_send()
            put_top(s, j).wait_send()
        for j in range(lane_tiles):
            out_copy(s, j).wait()


def step_call(n_ty, n_tx, scaling, *operands):
    obj, probe, phase, amplitude, _, _, tables, chosen = operands
    layers, _, tile, _ = obj.shape
    patch = probe.shape[1]
    slots = amplitude.shape[0]
    lane_tiles, strip_tiles = tile // LANES, patch // LANES
    all_tiles = lane_tiles + strip_tiles
    gets = 3 * strip_tiles + lane_tiles
    puts = 2 * strip_tiles + 2
    n_row, n_outer = n_ty // 2, n_tx // INNER
    row_rows = patch // n_row
    chunk = row_rows // n_outer
    sums = 2 * n_row + 2 * n_outer + INNER + 2
    vmem = pl.BlockSpec(memory_space=pltpu.VMEM)
    smem = pl.BlockSpec(memory_space=pltpu.SMEM)
    whole = pl.BlockSpec(memory_space=pl.ANY)
    return pl.pallas_call(
        functools.partial(step_kernel, n_ty, n_tx, scaling),
        name="step",
        out_shape=(
            jax.ShapeDtypeStruct(obj.shape, F32),
            jax.ShapeDtypeStruct((2, n_row, n_outer, chunk, patch), F32),
        ),
        in_specs=[whole, whole, whole, whole, smem, smem, whole, whole],
        out_specs=(whole, vmem),
        scratch_shapes=[
            pltpu.VMEM((2, all_tiles, tile + patch, LANES), F32),
            pltpu.VMEM((2, all_tiles, tile + patch, LANES), F32),
            pltpu.VMEM((slots, 2, strip_tiles + 1, 2 * tile + patch, LANES), F32),
            pltpu.VMEM((slots, 2, strip_tiles + 1, 2 * tile + patch, LANES), F32),
            pltpu.VMEM((layers, 2, all_tiles, tile + patch, LANES), F32),
            pltpu.VMEM((layers, 2, strip_tiles, tile, LANES), F32),
            pltpu.VMEM((layers, 2, all_tiles, patch, LANES), F32),
            pltpu.VMEM((slots, 2, patch, patch), F32),
            pltpu.VMEM((slots, 2, patch, patch), F32),
            pltpu.VMEM((2, patch, patch), F32),
            pltpu.VMEM((slots, patch, patch), F32),
            pltpu.VMEM((2, patch, patch), F32),
            pltpu.VMEM((patch, patch), F32),
            pltpu.VMEM((n_row, row_rows, patch), F32),
            pltpu.VMEM((n_row, row_rows, patch), F32),
            pltpu.VMEM((n_outer, chunk, patch), F32),
            pltpu.VMEM((n_outer, chunk, patch), F32),
            pltpu.VMEM((INNER, chunk, patch), F32),
            pltpu.VMEM(probe.shape, F32),
            pltpu.VMEM(phase.shape, F32),
            pltpu.VMEM(amplitude.shape, F32),
            pltpu.VMEM(tables.shape, BF16),
            pltpu.VMEM(chosen.shape, BF16),
            pltpu.SemaphoreType.DMA((layers, lane_tiles)),
            pltpu.SemaphoreType.DMA((5,)),
            pltpu.SemaphoreType.DMA((layers, gets)),
            pltpu.SemaphoreType.DMA((layers, gets)),
            pltpu.SemaphoreType.DMA((layers, puts)),
            pltpu.SemaphoreType.DMA((layers, puts)),
            pltpu.SemaphoreType.DMA((layers, lane_tiles)),
            pltpu.SemaphoreType.DMA((sums,)),
            pltpu.SemaphoreType.DMA((sums,)),
        ],
        compiler_params=pltpu.CompilerParams(
            collective_id=0, has_side_effects=True, vmem_limit_bytes=60 * 1024 * 1024
        ),
    )(*operands)


def solution(mesh):
    n_ty, n_tx = mesh.shape["ty"], mesh.shape["tx"]

    def per_device(object_field, probe_wave, prop_phase, amplitude, offsets, live_slots):
        patch = probe_wave.shape[1]
        scaling = 1.0 / math.sqrt(live_slots.shape[0] * n_ty * n_tx)
        owned, shared = step_call(
            n_ty,
            n_tx,
            scaling,
            object_field,
            probe_wave,
            prop_phase,
            amplitude,
            offsets,
            live_slots,
            jnp.asarray(dft_halves(patch)),
            jnp.asarray(even_odd(patch)),
        )
        return owned, shared.reshape(probe_wave.shape)

    placed = (
        P(None, None, "ty", "tx"),
        P(),
        P(),
        P(("ty", "tx"), None, None),
        P(None, ("ty", "tx")),
        P(("ty", "tx")),
    )
    return jax.shard_map(
        per_device,
        mesh=mesh,
        in_specs=placed,
        out_specs=(P(None, None, "ty", "tx"), P()),
        check_vma=False,
    )
```

```python
import functools
import math

import jax
import jax.numpy as jnp
import ml_dtypes
import numpy as np
from jax import lax
from jax.experimental import pallas as pl
from jax.experimental.pallas import tpu as pltpu
from jax.sharding import PartitionSpec as P

F32 = jnp.float32
BF16 = jnp.bfloat16
MESH = pl.DeviceIdType.MESH
LANES = 128
INNER = 4


def halves(table):
    high = table.astype(np.float32).astype(ml_dtypes.bfloat16)
    low = (table - high.astype(np.float64)).astype(ml_dtypes.bfloat16)
    return np.stack([high, low])


def dft_halves(length):
    half = length // 2
    sample = np.arange(half)[:, None]
    tables = []
    for parity in range(2):
        freq = 2 * np.arange(half)[None, :] + parity
        angle = 2.0 * math.pi * ((sample * freq) % length) / length
        cosine = np.cos(angle) / math.sqrt(length)
        sine = np.sin(angle) / math.sqrt(length)
        full = np.block([[cosine, -sine], [sine, cosine]])
        tables.append(np.stack([halves(full), halves(full.T)]))
    return np.stack(tables)


def even_odd(length):
    order = np.concatenate([np.arange(0, length, 2), np.arange(1, length, 2)])
    chosen = np.zeros((length, length), np.float32)
    chosen[order, np.arange(length)] = 1.0
    return np.stack([chosen, chosen.T]).astype(ml_dtypes.bfloat16)


def split(value):
    high = value.astype(BF16)
    low = (value - high.astype(F32)).astype(BF16)
    return high, low


def product(left, right):
    return jnp.dot(left, right, preferred_element_type=F32)


def from_right(value, table):
    high, low = split(value)
    left = jnp.concatenate([high, low, high], axis=1)
    return product(left, jnp.concatenate([table[0], table[0], table[1]], axis=0))


def from_left(table, value):
    high, low = split(value)
    right = jnp.concatenate([high, low, high], axis=0)
    return product(jnp.concatenate([table[0], table[0], table[1]], axis=1), right)


def thirds(value):
    high = value.astype(BF16)
    rest = value - high.astype(F32)
    middle = rest.astype(BF16)
    low = (rest - middle.astype(F32)).astype(BF16)
    return high, middle, low


def reorder(value, chosen, chosen_t):
    pieces = thirds(value)
    across = sum(product(piece, chosen) for piece in pieces)
    return sum(product(chosen_t, piece) for piece in thirds(across))


def beside(left, right):
    return jnp.concatenate([left, right], axis=1)


def above(top, bottom):
    return jnp.concatenate([top, bottom], axis=0)


def forward(real, imag, tables):
    n = LANES
    even = from_right(
        beside(real[:, :n] + real[:, n:], imag[:, :n] + imag[:, n:]), tables[0, 0]
    )
    odd = from_right(
        beside(real[:, :n] - real[:, n:], imag[:, :n] - imag[:, n:]), tables[1, 0]
    )
    real = beside(even[:, :n], odd[:, :n])
    imag = beside(even[:, n:], odd[:, n:])
    even = from_left(tables[0, 1], above(real[:n] + real[n:], imag[:n] + imag[n:]))
    odd = from_left(tables[1, 1], above(real[:n] - real[n:], imag[:n] - imag[n:]))
    return above(even[:n], odd[:n]), above(even[n:], odd[n:])


def backward(real, imag, tables):
    n = LANES
    even = from_left(tables[0, 0], above(real[:n], imag[:n]))
    odd = from_left(tables[1, 0], above(real[n:], imag[n:]))
    total, change = even + odd, even - odd
    real, imag = above(total[:n], change[:n]), above(total[n:], change[n:])
    even = from_right(beside(real[:, :n], imag[:, :n]), tables[0, 1])
    odd = from_right(beside(real[:, n:], imag[:, n:]), tables[1, 1])
    total, change = even + odd, even - odd
    return beside(total[:, :n], change[:, :n]), beside(total[:, n:], change[:, n:])


def step_kernel(
    n_ty,
    n_tx,
    scaling,
    obj,
    probe_given,
    phase_given,
    amplitude_given,
    offsets,
    live,
    tables_given,
    chosen_given,
    grad,
    probe_grad,
    wide_first,
    wide_second,
    padded_first,
    padded_second,
    total,
    from_left_tile,
    from_above,
    psi,
    trans,
    prop,
    target,
    probe_part,
    pair_part,
    pair_sums,
    row_part,
    row_sums,
    outer_part,
    inner_part,
    probe,
    phase,
    amplitude,
    tables,
    chosen,
    local_sem,
    given_sem,
    get_send,
    get_recv,
    put_send,
    put_recv,
    sum_send,
    sum_recv,
):
    wide = (wide_first, wide_second)
    padded = (padded_first, padded_second)
    layers, _, tile, _ = obj.shape
    patch = probe.shape[1]
    slots = amplitude.shape[0]
    lane_tiles = tile // LANES
    strip_tiles = patch // LANES
    all_tiles = lane_tiles + strip_tiles
    lower = tile - patch
    ty, tx = lax.axis_index("ty"), lax.axis_index("tx")
    left = (ty, lax.rem(tx + n_tx - 1, n_tx))
    right = (ty, lax.rem(tx + 1, n_tx))
    up = (lax.rem(ty + n_ty - 1, n_ty), tx)
    down = (lax.rem(ty + 1, n_ty), tx)

    n_row, n_outer = n_ty // 2, n_tx // INNER
    core, row = lax.rem(ty, 2), lax.div(ty, 2)
    inner, outer = lax.rem(tx, INNER), lax.div(tx, INNER)
    partner = (ty + 1 - 2 * core, tx)

    def outer_peer(step):
        index = lax.rem(outer + step, n_outer)
        return index, (ty, index * INNER + inner)

    def inner_peer(step):
        index = lax.rem(inner + step, INNER)
        return index, (ty, outer * INNER + index)

    def row_peer(step):
        index = lax.rem(row + step, n_row)
        return index, (index * 2 + core, tx)

    barrier = pltpu.get_barrier_semaphore()
    greeted = [left, right, up, down, partner]
    greeted += [outer_peer(step)[1] for step in range(1, n_outer)]
    greeted += [inner_peer(step)[1] for step in range(1, INNER)]
    greeted += [row_peer(step)[1] for step in range(1, n_row)]
    for device in greeted:
        pl.semaphore_signal(barrier, inc=1, device_id=device, device_id_type=MESH)
    pl.semaphore_wait(barrier, len(greeted))

    def remote(source, destination, send, recv, device):
        return pltpu.make_async_remote_copy(
            src_ref=source,
            dst_ref=destination,
            send_sem=send,
            recv_sem=recv,
            device_id=device,
            device_id_type=MESH,
        )

    def columns(j):
        return pl.ds(j * LANES, LANES)

    def get(s, source, destination, index, device):
        return remote(source, destination, get_send.at[s, index], get_recv.at[s, index], device)

    def get_right(s, block):
        first, size = ((0, patch), (patch, lower))[block]
        return [
            get(
                s,
                obj.at[s, :, pl.ds(first, size), columns(j)],
                wide[s].at[:, lane_tiles + j, pl.ds(first, size), :],
                block * strip_tiles + j,
                left,
            )
            for j in range(strip_tiles)
        ]

    def get_below(s):
        return [
            get(
                s,
                obj.at[s, :, pl.ds(0, patch), columns(j)],
                wide[s].at[:, j, pl.ds(tile, patch), :],
                2 * strip_tiles + j,
                up,
            )
            for j in range(lane_tiles)
        ]

    def get_corner(s, j):
        return get(
            s,
            wide[s].at[:, lane_tiles + j, pl.ds(0, patch), :],
            wide[s].at[:, lane_tiles + j, pl.ds(tile, patch), :],
            2 * strip_tiles + lane_tiles + j,
            up,
        )

    def relay_get(s):
        for j, copy in enumerate(get_right(s, 0)):
            copy.wait_recv()
            get_corner(s, j).start()

    def finish_get(s):
        for copy in get_right(s, 1) + get_below(s):
            copy.wait_recv()
        for j in range(strip_tiles):
            get_corner(s, j).wait_recv()

    def sent_get(s):
        for copy in get_right(s, 0) + get_right(s, 1) + get_below(s):
            copy.wait_send()

    def sent_corner(s):
        for j in range(strip_tiles):
            get_corner(s, j).wait_send()

    def put(s, source, destination, index, device):
        return remote(source, destination, put_send.at[s, index], put_recv.at[s, index], device)

    def put_corner(s, j):
        return put(
            s,
            total.at[s, :, lane_tiles + j, pl.ds(tile, patch), :],
            from_above.at[s, :, lane_tiles + j, :, :],
            j,
            down,
        )

    def put_top(s, j):
        return put(
            s,
            total.at[s, :, lane_tiles + j, pl.ds(0, patch), :],
            from_left_tile.at[s, :, j, pl.ds(0, patch), :],
            strip_tiles + j,
            right,
        )

    def put_bottom(s):
        return put(
            s,
            total.at[s, :, pl.ds(lane_tiles, strip_tiles), pl.ds(patch, lower), :],
            from_left_tile.at[s, :, :, pl.ds(patch, lower), :],
            2 * strip_tiles,
            right,
        )

    def put_below(s):
        return put(
            s,
            total.at[s, :, pl.ds(0, lane_tiles), pl.ds(tile, patch), :],
            from_above.at[s, :, pl.ds(0, lane_tiles), :, :],
            2 * strip_tiles + 1,
            down,
        )

    def start_corners(s):
        for j in range(strip_tiles):
            put_corner(s, j).start()

    def add_corner(s, j):
        put_corner(s, j).wait_recv()

        def add_rows(block, carry):
            rows = pl.ds(pl.multiple_of(block * 64, 64), 64)
            for part in range(2):
                total[s, part, lane_tiles + j, rows, :] += from_above[
                    s, part, lane_tiles + j, rows, :
                ]
            return carry

        lax.fori_loop(0, patch // 64, add_rows, 0)

    def finish_tile(s, j):
        if j < strip_tiles:
            put_top(s, j).wait_recv()

        def add_both(block, carry):
            rows = pl.ds(pl.multiple_of(block * 64, 64), 64)
            for part in range(2):
                value = total[s, part, j, rows, :] + from_above[s, part, j, rows, :]
                if j < strip_tiles:
                    value += from_left_tile[s, part, j, rows, :]
                grad[s, part, rows, columns(j)] = value
            return carry

        def add_left(block, carry):
            rows = pl.ds(pl.multiple_of(block * 64, 64), 64)
            for part in range(2):
                value = total[s, part, j, rows, :]
                if j < strip_tiles:
                    value += from_left_tile[s, part, j, rows, :]
                grad[s, part, rows, columns(j)] = value
            return carry

        lax.fori_loop(0, patch // 64, add_both, 0)
        lax.fori_loop(patch // 64, tile // 64, add_left, 0)

    def finish_put(s):
        put_bottom(s).wait_recv()
        put_below(s).wait_recv()
        for j in reversed(range(strip_tiles, lane_tiles)):
            finish_tile(s, j)
        for j in range(strip_tiles):
            finish_tile(s, j)

    def summed(source, destination, index, device):
        return remote(source, destination, sum_send.at[index], sum_recv.at[index], device)

    first_row = 1
    first_outer = first_row + n_row
    first_inner = first_outer + n_outer
    second_outer = first_inner + INNER
    second_row = second_outer + n_outer
    last_pair = second_row + n_row

    def stage(count, peer, base, mine, source, target_of):
        def sending(step):
            index, device = peer(step)
            return remote(
                source(index),
                target_of(mine),
                sum_send.at[base + index],
                sum_recv.at[base + mine],
                device,
            )

        def receiving(step):
            index, device = peer(step)
            return remote(
                source(index),
                target_of(index),
                sum_send.at[base + index],
                sum_recv.at[base + index],
                device,
            )

        def start():
            for step in range(1, count):
                sending(step).start()

        def finish():
            for step in range(1, count):
                receiving(step).wait_recv()

        def sent():
            for step in range(1, count):
                sending(step).wait_send()

        return start, finish, sent

    def pair_sum():
        return summed(probe_part.at[1 - core], pair_part, 0, partner)

    def pair_gather():
        return summed(probe_grad.at[core], probe_grad.at[core], last_pair, partner)

    def pair_arrival():
        return summed(probe_grad.at[1 - core], probe_grad.at[1 - core], last_pair, partner)

    row_sum = stage(
        n_row, row_peer, first_row, row,
        lambda index: pair_sums.at[index], lambda index: row_part.at[index],
    )
    outer_sum = stage(
        n_outer, outer_peer, first_outer, outer,
        lambda index: row_sums.at[index], lambda index: outer_part.at[index],
    )
    inner_sum = stage(
        INNER, inner_peer, first_inner, inner,
        lambda index: inner_part.at[inner], lambda index: inner_part.at[index],
    )
    outer_gather = stage(
        n_outer, outer_peer, second_outer, outer,
        lambda index: probe_grad.at[core, row, outer],
        lambda index: probe_grad.at[core, row, index],
    )
    row_gather = stage(
        n_row, row_peer, second_row, row,
        lambda index: probe_grad.at[core, row],
        lambda index: probe_grad.at[core, index],
    )

    def reduced(parts, count):
        value = parts[0]
        for index in range(1, count):
            value += parts[index]
        return value

    def after_pair():
        pair_sum().wait_recv()
        size = pair_sums.shape[1]
        for index in range(n_row):
            rows = pl.ds(index * size, size)
            pair_sums[index] = probe_part[core, rows, :] + pair_part[rows, :]
        row_part[row] = pair_sums[row]
        row_sum[0]()

    def after_row():
        row_sum[1]()
        size = row_sums.shape[1]
        for index in range(n_outer):
            rows = pl.ds(index * size, size)
            value = row_part[0, rows, :]
            for other in range(1, n_row):
                value += row_part[other, rows, :]
            row_sums[index] = value
        outer_part[outer] = row_sums[outer]
        outer_sum[0]()

    def after_outer():
        outer_sum[1]()
        inner_part[inner] = reduced(outer_part, n_outer)
        inner_sum[0]()

    def after_inner():
        inner_sum[1]()
        probe_grad[core, row, outer] = reduced(inner_part, INNER) * scaling
        outer_gather[0]()

    def after_outer_gather():
        outer_gather[1]()
        row_gather[0]()

    def after_row_gather():
        row_gather[1]()
        pair_gather().start()

    def finish_sum():
        pair_arrival().wait_recv()
        pair_gather().wait_send()
        pair_sum().wait_send()
        for part in (row_sum, outer_sum, inner_sum, outer_gather, row_gather):
            part[2]()

    for copy in get_right(0, 0) + get_below(0) + get_right(0, 1):
        copy.start()
    local = [
        pltpu.make_async_copy(
            obj.at[s, :, :, columns(j)], wide[s].at[:, j, pl.ds(0, tile), :], local_sem.at[s, j]
        )
        for s in range(layers)
        for j in range(lane_tiles)
    ]
    given = [
        pltpu.make_async_copy(source, destination, given_sem.at[index])
        for index, (source, destination) in enumerate(
            (
                (chosen_given, chosen),
                (phase_given, phase),
                (amplitude_given, amplitude),
                (probe_given, probe),
                (tables_given, tables),
            )
        )
    ]
    for copy in given + local:
        copy.start()

    def clear(q, carry):
        margin = jnp.zeros((tile, LANES), F32)
        for s in range(layers):
            for part in range(2):
                for j in range(strip_tiles + 1):
                    padded[s][q, part, j, pl.ds(0, tile), :] = margin
                    padded[s][q, part, j, pl.ds(tile + patch, tile), :] = margin
        return carry

    lax.fori_loop(0, slots, clear, 0)
    for copy in given:
        copy.wait()

    def order_target(q, carry):
        target[q] = reorder(amplitude[q], chosen[0], chosen[1])
        return carry

    lax.fori_loop(0, slots, order_target, 0)
    angle = reorder(phase[...], chosen[0], chosen[1])
    prop[0] = jnp.cos(angle)
    prop[1] = jnp.sin(angle)
    for copy in local:
        copy.wait()
    relay_get(0)
    for copy in get_right(1, 0):
        copy.start()
    finish_get(0)
    for copy in get_below(1) + get_right(1, 1):
        copy.start()
    sent_get(0)

    lane = lax.broadcasted_iota(jnp.int32, (patch, LANES), 1)

    def place(q):
        row, column = offsets[0, q], offsets[1, q]
        return row, lax.shift_right_logical(column, 7), lax.bitwise_and(column, LANES - 1)

    def window(s, part, q):
        row, tile_index, shift = place(q)
        back = lax.bitwise_and(LANES - shift, LANES - 1)
        rolled = [
            pltpu.roll(wide[s][part, tile_index + k, pl.ds(row, patch), :], back, 1)
            for k in range(strip_tiles + 1)
        ]
        keep = lane < LANES - shift
        return jnp.concatenate(
            [jnp.where(keep, rolled[k], rolled[k + 1]) for k in range(strip_tiles)], axis=1
        )

    def deposit(s, q, part, piece):
        _, _, shift = place(q)
        rolled = [
            pltpu.roll(piece[:, k * LANES : (k + 1) * LANES], shift, 1) for k in range(strip_tiles)
        ]
        rolled = [jnp.zeros((patch, LANES), F32)] + rolled + [jnp.zeros((patch, LANES), F32)]
        keep = lane >= shift
        for k in range(strip_tiles + 1):
            padded[s][q, part, k, pl.ds(tile, patch), :] = jnp.where(keep, rolled[k + 1], rolled[k])

    def gather(s, tiles, first, size):
        places = [place(q) for q in range(slots)]
        alive = [live[q].astype(F32) for q in range(slots)]

        def rows_of(block, carry):
            begin = first + block * 64
            for j in tiles:
                weights, sources = [], []
                for q in range(slots):
                    inside = j - places[q][1]
                    valid = jnp.logical_and(inside >= 0, inside <= strip_tiles)
                    weights.append(jnp.where(valid, alive[q], 0.0))
                    sources.append(jnp.clip(inside, 0, strip_tiles))
                for part in range(2):
                    value = jnp.zeros((64, LANES), F32)
                    for q in range(slots):
                        rows = pl.ds(tile - places[q][0] + begin, 64)
                        value += weights[q] * padded[s][q, part, sources[q], rows, :]
                    total[s, part, j, pl.ds(pl.multiple_of(begin, 64), 64), :] = value
            return carry

        lax.fori_loop(0, size // 64, rows_of, 0)

    def first_layer(q, carry):
        trans_real, trans_imag = window(0, 0, q), window(0, 1, q)
        trans[q, 0], trans[q, 1] = trans_real, trans_imag
        freq_real, freq_imag = forward(
            trans_real * probe[0] - trans_imag * probe[1],
            trans_real * probe[1] + trans_imag * probe[0],
            tables,
        )
        psi[q, 0], psi[q, 1] = backward(
            prop[0] * freq_real - prop[1] * freq_imag,
            prop[0] * freq_imag + prop[1] * freq_real,
            tables,
        )
        return carry

    lax.fori_loop(0, slots, first_layer, 0)
    sent_corner(0)
    relay_get(1)
    sent_get(1)
    finish_get(1)
    sent_corner(1)

    def second_layer(q, carry):
        trans_real, trans_imag = window(1, 0, q), window(1, 1, q)
        wave_real, wave_imag = psi[q, 0], psi[q, 1]
        freq_real, freq_imag = forward(
            trans_real * wave_real - trans_imag * wave_imag,
            trans_real * wave_imag + trans_imag * wave_real,
            tables,
        )
        energy = freq_real * freq_real + freq_imag * freq_imag + 0.25
        factor = target[q] / jnp.sqrt(energy) - 1.0
        back_real, back_imag = backward(freq_real * factor, freq_imag * factor, tables)
        wave_real, wave_imag = psi[q, 0], psi[q, 1]
        deposit(1, q, 0, wave_real * back_real + wave_imag * back_imag)
        deposit(1, q, 1, wave_real * back_imag - wave_imag * back_real)
        trans_real, trans_imag = window(1, 0, q), window(1, 1, q)
        psi[q, 0] = trans_real * back_real + trans_imag * back_imag
        psi[q, 1] = trans_real * back_imag - trans_imag * back_real
        return carry

    for q in range(slots):
        second_layer(q, 0)
    strip = range(lane_tiles, all_tiles)
    own = range(lane_tiles)

    gather(1, strip, 0, tile + patch)
    start_corners(1)
    put_bottom(1).start()
    gather(1, own, tile, patch)
    probe_part[...] = jnp.zeros(probe_part.shape, F32)

    def third_layer(q, carry):
        freq_real, freq_imag = forward(psi[q, 0], psi[q, 1], tables)
        back_real, back_imag = backward(
            prop[0] * freq_real + prop[1] * freq_imag,
            prop[0] * freq_imag - prop[1] * freq_real,
            tables,
        )
        deposit(0, q, 0, probe[0] * back_real + probe[1] * back_imag)
        deposit(0, q, 1, probe[0] * back_imag - probe[1] * back_real)
        weight = live[q].astype(F32)
        probe_part[0] += weight * (trans[q, 0] * back_real + trans[q, 1] * back_imag)
        probe_part[1] += weight * (trans[q, 0] * back_imag - trans[q, 1] * back_real)
        return carry

    for q in range(slots):
        third_layer(q, 0)
    pair_sum().start()
    for j in range(strip_tiles):
        add_corner(1, j)
    after_pair()
    put_top(1, 0).start()
    gather(0, strip, 0, tile + patch)
    start_corners(0)
    put_below(1).start()
    gather(0, own, tile, patch)
    gather(1, own, 0, tile)
    after_row()
    put_top(1, 1).start()
    gather(0, own, 0, tile)
    after_outer()
    put_bottom(0).start()
    add_corner(0, 0)
    after_inner()
    put_top(0, 0).start()
    add_corner(0, 1)
    after_outer_gather()
    put_top(0, 1).start()
    put_below(0).start()
    finish_put(1)
    after_row_gather()
    finish_put(0)
    finish_sum()
    for s in range(layers):
        put_bottom(s).wait_send()
        put_below(s).wait_send()
        for j in range(strip_tiles):
            put_corner(s, j).wait_send()
            put_top(s, j).wait_send()


def step_call(n_ty, n_tx, scaling, *operands):
    obj, probe, phase, amplitude, _, _, tables, chosen = operands
    layers, _, tile, _ = obj.shape
    patch = probe.shape[1]
    slots = amplitude.shape[0]
    lane_tiles, strip_tiles = tile // LANES, patch // LANES
    all_tiles = lane_tiles + strip_tiles
    gets = 3 * strip_tiles + lane_tiles
    puts = 2 * strip_tiles + 2
    n_row, n_outer = n_ty // 2, n_tx // INNER
    row_rows = patch // n_row
    chunk = row_rows // n_outer
    sums = 2 * n_row + 2 * n_outer + INNER + 2
    vmem = pl.BlockSpec(memory_space=pltpu.VMEM)
    smem = pl.BlockSpec(memory_space=pltpu.SMEM)
    whole = pl.BlockSpec(memory_space=pl.ANY)
    return pl.pallas_call(
        functools.partial(step_kernel, n_ty, n_tx, scaling),
        name="step",
        out_shape=(
            pltpu.VMEM(obj.shape, F32),
            pltpu.VMEM((2, n_row, n_outer, chunk, patch), F32),
        ),
        in_specs=[whole, whole, whole, whole, smem, smem, whole, whole],
        out_specs=(vmem, vmem),
        scratch_shapes=[
            pltpu.VMEM((2, all_tiles, tile + patch, LANES), F32),
            pltpu.VMEM((2, all_tiles, tile + patch, LANES), F32),
            pltpu.VMEM((slots, 2, strip_tiles + 1, 2 * tile + patch, LANES), F32),
            pltpu.VMEM((slots, 2, strip_tiles + 1, 2 * tile + patch, LANES), F32),
            pltpu.VMEM((layers, 2, all_tiles, tile + patch, LANES), F32),
            pltpu.VMEM((layers, 2, strip_tiles, tile, LANES), F32),
            pltpu.VMEM((layers, 2, all_tiles, patch, LANES), F32),
            pltpu.VMEM((slots, 2, patch, patch), F32),
            pltpu.VMEM((slots, 2, patch, patch), F32),
            pltpu.VMEM((2, patch, patch), F32),
            pltpu.VMEM((slots, patch, patch), F32),
            pltpu.VMEM((2, patch, patch), F32),
            pltpu.VMEM((patch, patch), F32),
            pltpu.VMEM((n_row, row_rows, patch), F32),
            pltpu.VMEM((n_row, row_rows, patch), F32),
            pltpu.VMEM((n_outer, chunk, patch), F32),
            pltpu.VMEM((n_outer, chunk, patch), F32),
            pltpu.VMEM((INNER, chunk, patch), F32),
            pltpu.VMEM(probe.shape, F32),
            pltpu.VMEM(phase.shape, F32),
            pltpu.VMEM(amplitude.shape, F32),
            pltpu.VMEM(tables.shape, BF16),
            pltpu.VMEM(chosen.shape, BF16),
            pltpu.SemaphoreType.DMA((layers, lane_tiles)),
            pltpu.SemaphoreType.DMA((5,)),
            pltpu.SemaphoreType.DMA((layers, gets)),
            pltpu.SemaphoreType.DMA((layers, gets)),
            pltpu.SemaphoreType.DMA((layers, puts)),
            pltpu.SemaphoreType.DMA((layers, puts)),
            pltpu.SemaphoreType.DMA((sums,)),
            pltpu.SemaphoreType.DMA((sums,)),
        ],
        compiler_params=pltpu.CompilerParams(
            collective_id=0, has_side_effects=True, vmem_limit_bytes=57 * 1024 * 1024
        ),
    )(*operands)


def copy_kernel(grad, shared, grad_out, shared_out, sem):
    copies = [
        pltpu.make_async_copy(grad.at[s, part], grad_out.at[s, part], sem.at[2 * s + part])
        for s in range(grad.shape[0])
        for part in range(2)
    ]
    copies.append(pltpu.make_async_copy(shared, shared_out, sem.at[len(copies)]))
    for copy in copies:
        copy.start()
    for copy in copies:
        copy.wait()


def copy_call(grad, shared):
    whole = pl.BlockSpec(memory_space=pl.ANY)
    vmem = pl.BlockSpec(memory_space=pltpu.VMEM)
    return pl.pallas_call(
        copy_kernel,
        name="hand_over",
        out_shape=(
            jax.ShapeDtypeStruct(grad.shape, F32),
            jax.ShapeDtypeStruct(shared.shape, F32),
        ),
        in_specs=[vmem, vmem],
        out_specs=(whole, whole),
        scratch_shapes=[pltpu.SemaphoreType.DMA((2 * grad.shape[0] + 1,))],
    )(grad, shared)


def solution(mesh):
    n_ty, n_tx = mesh.shape["ty"], mesh.shape["tx"]

    def per_device(object_field, probe_wave, prop_phase, amplitude, offsets, live_slots):
        patch = probe_wave.shape[1]
        scaling = 1.0 / math.sqrt(live_slots.shape[0] * n_ty * n_tx)
        owned, shared = step_call(
            n_ty,
            n_tx,
            scaling,
            object_field,
            probe_wave,
            prop_phase,
            amplitude,
            offsets,
            live_slots,
            jnp.asarray(dft_halves(patch)),
            jnp.asarray(even_odd(patch)),
        )
        owned = pltpu.with_memory_space_constraint(owned, pltpu.VMEM)
        shared = pltpu.with_memory_space_constraint(shared, pltpu.VMEM)
        owned, shared = copy_call(owned, shared)
        return owned, shared.reshape(probe_wave.shape)

    placed = (
        P(None, None, "ty", "tx"),
        P(),
        P(),
        P(("ty", "tx"), None, None),
        P(None, ("ty", "tx")),
        P(("ty", "tx")),
    )
    return jax.shard_map(
        per_device,
        mesh=mesh,
        in_specs=placed,
        out_specs=(P(None, None, "ty", "tx"), P()),
        check_vma=False,
    )
```

```python
import functools
import math

import jax
import jax.numpy as jnp
import ml_dtypes
import numpy as np
from jax import lax
from jax.experimental import pallas as pl
from jax.experimental.pallas import tpu as pltpu
from jax.sharding import PartitionSpec as P

F32 = jnp.float32
BF16 = jnp.bfloat16
MESH = pl.DeviceIdType.MESH
LANES = 128
INNER = 4


def halves(table):
    high = table.astype(np.float32).astype(ml_dtypes.bfloat16)
    low = (table - high.astype(np.float64)).astype(ml_dtypes.bfloat16)
    return np.stack([high, low])


def dft_halves(length):
    half = length // 2
    sample = np.arange(half)[:, None]
    tables = []
    for parity in range(2):
        freq = 2 * np.arange(half)[None, :] + parity
        angle = 2.0 * math.pi * ((sample * freq) % length) / length
        cosine = np.cos(angle) / math.sqrt(length)
        sine = np.sin(angle) / math.sqrt(length)
        full = np.block([[cosine, -sine], [sine, cosine]])
        tables.append(np.stack([halves(full), halves(full.T)]))
    return np.stack(tables)


def even_odd(length):
    order = np.concatenate([np.arange(0, length, 2), np.arange(1, length, 2)])
    chosen = np.zeros((length, length), np.float32)
    chosen[order, np.arange(length)] = 1.0
    return np.stack([chosen, chosen.T]).astype(ml_dtypes.bfloat16)


def split(value):
    high = value.astype(BF16)
    low = (value - high.astype(F32)).astype(BF16)
    return high, low


def product(left, right):
    return jnp.dot(left, right, preferred_element_type=F32)


def from_right(value, table):
    high, low = split(value)
    left = jnp.concatenate([high, low, high], axis=1)
    return product(left, jnp.concatenate([table[0], table[0], table[1]], axis=0))


def from_left(table, value):
    high, low = split(value)
    right = jnp.concatenate([high, low, high], axis=0)
    return product(jnp.concatenate([table[0], table[0], table[1]], axis=1), right)


def thirds(value):
    high = value.astype(BF16)
    rest = value - high.astype(F32)
    middle = rest.astype(BF16)
    low = (rest - middle.astype(F32)).astype(BF16)
    return high, middle, low


def reorder(value, chosen, chosen_t):
    pieces = thirds(value)
    across = sum(product(piece, chosen) for piece in pieces)
    return sum(product(chosen_t, piece) for piece in thirds(across))


def beside(left, right):
    return jnp.concatenate([left, right], axis=1)


def above(top, bottom):
    return jnp.concatenate([top, bottom], axis=0)


def forward(real, imag, tables):
    n = LANES
    even = from_right(
        beside(real[:, :n] + real[:, n:], imag[:, :n] + imag[:, n:]), tables[0, 0]
    )
    odd = from_right(
        beside(real[:, :n] - real[:, n:], imag[:, :n] - imag[:, n:]), tables[1, 0]
    )
    real = beside(even[:, :n], odd[:, :n])
    imag = beside(even[:, n:], odd[:, n:])
    even = from_left(tables[0, 1], above(real[:n] + real[n:], imag[:n] + imag[n:]))
    odd = from_left(tables[1, 1], above(real[:n] - real[n:], imag[:n] - imag[n:]))
    return above(even[:n], odd[:n]), above(even[n:], odd[n:])


def backward(real, imag, tables):
    n = LANES
    even = from_left(tables[0, 0], above(real[:n], imag[:n]))
    odd = from_left(tables[1, 0], above(real[n:], imag[n:]))
    total, change = even + odd, even - odd
    real, imag = above(total[:n], change[:n]), above(total[n:], change[n:])
    even = from_right(beside(real[:, :n], imag[:, :n]), tables[0, 1])
    odd = from_right(beside(real[:, n:], imag[:, n:]), tables[1, 1])
    total, change = even + odd, even - odd
    return beside(total[:, :n], change[:, :n]), beside(total[:, n:], change[:, n:])


def step_kernel(
    n_ty,
    n_tx,
    scaling,
    obj,
    probe_given,
    phase_given,
    amplitude_given,
    offsets,
    live,
    tables_given,
    chosen_given,
    grad,
    probe_grad,
    wide_first,
    wide_second,
    padded_first,
    padded_second,
    total,
    from_left_tile,
    from_above,
    psi,
    trans,
    prop,
    target,
    probe_part,
    pair_part,
    pair_sums,
    row_part,
    row_sums,
    outer_part,
    inner_part,
    probe,
    phase,
    amplitude,
    tables,
    chosen,
    local_sem,
    given_sem,
    get_send,
    get_recv,
    put_send,
    put_recv,
    sum_send,
    sum_recv,
):
    wide = (wide_first, wide_second)
    padded = (padded_first, padded_second)
    layers, _, tile, _ = obj.shape
    patch = probe.shape[1]
    slots = amplitude.shape[0]
    lane_tiles = tile // LANES
    strip_tiles = patch // LANES
    all_tiles = lane_tiles + strip_tiles
    lower = tile - patch
    ty, tx = lax.axis_index("ty"), lax.axis_index("tx")
    left = (ty, lax.rem(tx + n_tx - 1, n_tx))
    right = (ty, lax.rem(tx + 1, n_tx))
    up = (lax.rem(ty + n_ty - 1, n_ty), tx)
    down = (lax.rem(ty + 1, n_ty), tx)

    n_row, n_outer = n_ty // 2, n_tx // INNER
    core, row = lax.rem(ty, 2), lax.div(ty, 2)
    inner, outer = lax.rem(tx, INNER), lax.div(tx, INNER)
    partner = (ty + 1 - 2 * core, tx)

    def outer_peer(step):
        index = lax.rem(outer + step, n_outer)
        return index, (ty, index * INNER + inner)

    def inner_peer(step):
        index = lax.rem(inner + step, INNER)
        return index, (ty, outer * INNER + index)

    def row_peer(step):
        index = lax.rem(row + step, n_row)
        return index, (index * 2 + core, tx)

    barrier = pltpu.get_barrier_semaphore()
    greeted = [left, right, up, down, partner]
    greeted += [outer_peer(step)[1] for step in range(1, n_outer)]
    greeted += [inner_peer(step)[1] for step in range(1, INNER)]
    greeted += [row_peer(step)[1] for step in range(1, n_row)]
    for device in greeted:
        pl.semaphore_signal(barrier, inc=1, device_id=device, device_id_type=MESH)
    pl.semaphore_wait(barrier, len(greeted))

    def remote(source, destination, send, recv, device):
        return pltpu.make_async_remote_copy(
            src_ref=source,
            dst_ref=destination,
            send_sem=send,
            recv_sem=recv,
            device_id=device,
            device_id_type=MESH,
        )

    def columns(j):
        return pl.ds(j * LANES, LANES)

    def get(s, source, destination, index, device):
        return remote(source, destination, get_send.at[s, index], get_recv.at[s, index], device)

    def get_right(s, block):
        first, size = ((0, patch), (patch, lower))[block]
        return [
            get(
                s,
                obj.at[s, :, pl.ds(first, size), columns(j)],
                wide[s].at[:, lane_tiles + j, pl.ds(first, size), :],
                block * strip_tiles + j,
                left,
            )
            for j in range(strip_tiles)
        ]

    def get_below(s):
        return [
            get(
                s,
                obj.at[s, :, pl.ds(0, patch), columns(j)],
                wide[s].at[:, j, pl.ds(tile, patch), :],
                2 * strip_tiles + j,
                up,
            )
            for j in range(lane_tiles)
        ]

    def get_corner(s, j):
        return get(
            s,
            wide[s].at[:, lane_tiles + j, pl.ds(0, patch), :],
            wide[s].at[:, lane_tiles + j, pl.ds(tile, patch), :],
            2 * strip_tiles + lane_tiles + j,
            up,
        )

    def relay_get(s):
        for j, copy in enumerate(get_right(s, 0)):
            copy.wait_recv()
            get_corner(s, j).start()

    def finish_get(s):
        for copy in get_right(s, 1) + get_below(s):
            copy.wait_recv()
        for j in range(strip_tiles):
            get_corner(s, j).wait_recv()

    def sent_get(s):
        for copy in get_right(s, 0) + get_right(s, 1) + get_below(s):
            copy.wait_send()

    def sent_corner(s):
        for j in range(strip_tiles):
            get_corner(s, j).wait_send()

    def put(s, source, destination, index, device):
        return remote(source, destination, put_send.at[s, index], put_recv.at[s, index], device)

    def put_corner(s, j):
        return put(
            s,
            total.at[s, :, lane_tiles + j, pl.ds(tile, patch), :],
            from_above.at[s, :, lane_tiles + j, :, :],
            j,
            down,
        )

    def put_top(s, j):
        return put(
            s,
            total.at[s, :, lane_tiles + j, pl.ds(0, patch), :],
            from_left_tile.at[s, :, j, pl.ds(0, patch), :],
            strip_tiles + j,
            right,
        )

    def put_bottom(s):
        return put(
            s,
            total.at[s, :, pl.ds(lane_tiles, strip_tiles), pl.ds(patch, lower), :],
            from_left_tile.at[s, :, :, pl.ds(patch, lower), :],
            2 * strip_tiles,
            right,
        )

    def put_below(s):
        return put(
            s,
            total.at[s, :, pl.ds(0, lane_tiles), pl.ds(tile, patch), :],
            from_above.at[s, :, pl.ds(0, lane_tiles), :, :],
            2 * strip_tiles + 1,
            down,
        )

    def start_corners(s):
        for j in range(strip_tiles):
            put_corner(s, j).start()

    def add_corner(s, j):
        put_corner(s, j).wait_recv()

        def add_rows(block, carry):
            rows = pl.ds(pl.multiple_of(block * 64, 64), 64)
            for part in range(2):
                total[s, part, lane_tiles + j, rows, :] += from_above[
                    s, part, lane_tiles + j, rows, :
                ]
            return carry

        lax.fori_loop(0, patch // 64, add_rows, 0)

    def finish_tile(s, j):
        if j < strip_tiles:
            put_top(s, j).wait_recv()

        def add_both(block, carry):
            rows = pl.ds(pl.multiple_of(block * 64, 64), 64)
            for part in range(2):
                value = total[s, part, j, rows, :] + from_above[s, part, j, rows, :]
                if j < strip_tiles:
                    value += from_left_tile[s, part, j, rows, :]
                grad[s, part, rows, columns(j)] = value
            return carry

        def add_left(block, carry):
            rows = pl.ds(pl.multiple_of(block * 64, 64), 64)
            for part in range(2):
                value = total[s, part, j, rows, :]
                if j < strip_tiles:
                    value += from_left_tile[s, part, j, rows, :]
                grad[s, part, rows, columns(j)] = value
            return carry

        lax.fori_loop(0, patch // 64, add_both, 0)
        lax.fori_loop(patch // 64, tile // 64, add_left, 0)

    def finish_put(s):
        put_bottom(s).wait_recv()
        put_below(s).wait_recv()
        for j in reversed(range(strip_tiles, lane_tiles)):
            finish_tile(s, j)
        for j in range(strip_tiles):
            finish_tile(s, j)

    def summed(source, destination, index, device):
        return remote(source, destination, sum_send.at[index], sum_recv.at[index], device)

    first_row = 1
    first_outer = first_row + n_row
    first_inner = first_outer + n_outer
    second_outer = first_inner + INNER
    second_row = second_outer + n_outer
    last_pair = second_row + n_row

    def stage(count, peer, base, mine, source, target_of):
        def sending(step):
            index, device = peer(step)
            return remote(
                source(index),
                target_of(mine),
                sum_send.at[base + index],
                sum_recv.at[base + mine],
                device,
            )

        def receiving(step):
            index, device = peer(step)
            return remote(
                source(index),
                target_of(index),
                sum_send.at[base + index],
                sum_recv.at[base + index],
                device,
            )

        def start():
            for step in range(1, count):
                sending(step).start()

        def finish():
            for step in range(1, count):
                receiving(step).wait_recv()

        def sent():
            for step in range(1, count):
                sending(step).wait_send()

        return start, finish, sent

    def pair_sum():
        return summed(probe_part.at[1 - core], pair_part, 0, partner)

    def pair_gather():
        return summed(probe_grad.at[core], probe_grad.at[core], last_pair, partner)

    def pair_arrival():
        return summed(probe_grad.at[1 - core], probe_grad.at[1 - core], last_pair, partner)

    row_sum = stage(
        n_row, row_peer, first_row, row,
        lambda index: pair_sums.at[index], lambda index: row_part.at[index],
    )
    outer_sum = stage(
        n_outer, outer_peer, first_outer, outer,
        lambda index: row_sums.at[index], lambda index: outer_part.at[index],
    )
    inner_sum = stage(
        INNER, inner_peer, first_inner, inner,
        lambda index: inner_part.at[inner], lambda index: inner_part.at[index],
    )
    outer_gather = stage(
        n_outer, outer_peer, second_outer, outer,
        lambda index: probe_grad.at[core, row, outer],
        lambda index: probe_grad.at[core, row, index],
    )
    row_gather = stage(
        n_row, row_peer, second_row, row,
        lambda index: probe_grad.at[core, row],
        lambda index: probe_grad.at[core, index],
    )

    def reduced(parts, count):
        value = parts[0]
        for index in range(1, count):
            value += parts[index]
        return value

    def after_pair():
        pair_sum().wait_recv()
        size = pair_sums.shape[1]
        for index in range(n_row):
            rows = pl.ds(index * size, size)
            pair_sums[index] = probe_part[core, rows, :] + pair_part[rows, :]
        row_part[row] = pair_sums[row]
        row_sum[0]()

    def after_row():
        row_sum[1]()
        size = row_sums.shape[1]
        for index in range(n_outer):
            rows = pl.ds(index * size, size)
            value = row_part[0, rows, :]
            for other in range(1, n_row):
                value += row_part[other, rows, :]
            row_sums[index] = value
        outer_part[outer] = row_sums[outer]
        outer_sum[0]()

    def after_outer():
        outer_sum[1]()
        inner_part[inner] = reduced(outer_part, n_outer)
        inner_sum[0]()

    def after_inner():
        inner_sum[1]()
        probe_grad[core, row, outer] = reduced(inner_part, INNER) * scaling
        outer_gather[0]()

    def after_outer_gather():
        outer_gather[1]()
        row_gather[0]()

    def after_row_gather():
        row_gather[1]()
        pair_gather().start()

    def finish_sum():
        pair_arrival().wait_recv()
        pair_gather().wait_send()
        pair_sum().wait_send()
        for part in (row_sum, outer_sum, inner_sum, outer_gather, row_gather):
            part[2]()

    for copy in get_right(0, 0) + get_below(0) + get_right(0, 1):
        copy.start()
    local = [
        pltpu.make_async_copy(
            obj.at[s, :, :, columns(j)], wide[s].at[:, j, pl.ds(0, tile), :], local_sem.at[s, j]
        )
        for s in range(layers)
        for j in range(lane_tiles)
    ]
    given = [
        pltpu.make_async_copy(source, destination, given_sem.at[index])
        for index, (source, destination) in enumerate(
            (
                (chosen_given, chosen),
                (phase_given, phase),
                (amplitude_given, amplitude),
                (probe_given, probe),
                (tables_given, tables),
            )
        )
    ]
    for copy in given + local:
        copy.start()

    def clear(q, carry):
        margin = jnp.zeros((tile, LANES), F32)
        for s in range(layers):
            for part in range(2):
                for j in range(strip_tiles + 1):
                    padded[s][q, part, j, pl.ds(0, tile), :] = margin
                    padded[s][q, part, j, pl.ds(tile + patch, tile), :] = margin
        return carry

    lax.fori_loop(0, slots, clear, 0)
    for copy in given:
        copy.wait()

    def order_target(q, carry):
        target[q] = reorder(amplitude[q], chosen[0], chosen[1])
        return carry

    lax.fori_loop(0, slots, order_target, 0)
    angle = reorder(phase[...], chosen[0], chosen[1])
    prop[0] = jnp.cos(angle)
    prop[1] = jnp.sin(angle)
    for copy in local:
        copy.wait()
    relay_get(0)
    for copy in get_right(1, 0):
        copy.start()
    finish_get(0)
    for copy in get_below(1) + get_right(1, 1):
        copy.start()
    sent_get(0)

    lane = lax.broadcasted_iota(jnp.int32, (patch, LANES), 1)

    def place(q):
        row, column = offsets[0, q], offsets[1, q]
        return row, lax.shift_right_logical(column, 7), lax.bitwise_and(column, LANES - 1)

    def window(s, part, q):
        row, tile_index, shift = place(q)
        back = lax.bitwise_and(LANES - shift, LANES - 1)
        rolled = [
            pltpu.roll(wide[s][part, tile_index + k, pl.ds(row, patch), :], back, 1)
            for k in range(strip_tiles + 1)
        ]
        keep = lane < LANES - shift
        return jnp.concatenate(
            [jnp.where(keep, rolled[k], rolled[k + 1]) for k in range(strip_tiles)], axis=1
        )

    def deposit(s, q, part, piece):
        _, _, shift = place(q)
        rolled = [
            pltpu.roll(piece[:, k * LANES : (k + 1) * LANES], shift, 1) for k in range(strip_tiles)
        ]
        rolled = [jnp.zeros((patch, LANES), F32)] + rolled + [jnp.zeros((patch, LANES), F32)]
        keep = lane >= shift
        for k in range(strip_tiles + 1):
            padded[s][q, part, k, pl.ds(tile, patch), :] = jnp.where(keep, rolled[k + 1], rolled[k])

    def gather(s, tiles, first, size):
        places = [place(q) for q in range(slots)]
        alive = [live[q].astype(F32) for q in range(slots)]

        def rows_of(block, carry):
            begin = first + block * 64
            for j in tiles:
                weights, sources = [], []
                for q in range(slots):
                    inside = j - places[q][1]
                    valid = jnp.logical_and(inside >= 0, inside <= strip_tiles)
                    weights.append(jnp.where(valid, alive[q], 0.0))
                    sources.append(jnp.clip(inside, 0, strip_tiles))
                for part in range(2):
                    value = jnp.zeros((64, LANES), F32)
                    for q in range(slots):
                        rows = pl.ds(tile - places[q][0] + begin, 64)
                        value += weights[q] * padded[s][q, part, sources[q], rows, :]
                    total[s, part, j, pl.ds(pl.multiple_of(begin, 64), 64), :] = value
            return carry

        lax.fori_loop(0, size // 64, rows_of, 0)

    def first_layer(q, carry):
        trans_real, trans_imag = window(0, 0, q), window(0, 1, q)
        trans[q, 0], trans[q, 1] = trans_real, trans_imag
        freq_real, freq_imag = forward(
            trans_real * probe[0] - trans_imag * probe[1],
            trans_real * probe[1] + trans_imag * probe[0],
            tables,
        )
        psi[q, 0], psi[q, 1] = backward(
            prop[0] * freq_real - prop[1] * freq_imag,
            prop[0] * freq_imag + prop[1] * freq_real,
            tables,
        )
        return carry

    lax.fori_loop(0, slots, first_layer, 0)
    sent_corner(0)
    relay_get(1)
    sent_get(1)
    finish_get(1)
    sent_corner(1)

    def second_layer(q, carry):
        trans_real, trans_imag = window(1, 0, q), window(1, 1, q)
        wave_real, wave_imag = psi[q, 0], psi[q, 1]
        freq_real, freq_imag = forward(
            trans_real * wave_real - trans_imag * wave_imag,
            trans_real * wave_imag + trans_imag * wave_real,
            tables,
        )
        energy = freq_real * freq_real + freq_imag * freq_imag + 0.25
        factor = target[q] / jnp.sqrt(energy) - 1.0
        back_real, back_imag = backward(freq_real * factor, freq_imag * factor, tables)
        wave_real, wave_imag = psi[q, 0], psi[q, 1]
        deposit(1, q, 0, wave_real * back_real + wave_imag * back_imag)
        deposit(1, q, 1, wave_real * back_imag - wave_imag * back_real)
        trans_real, trans_imag = window(1, 0, q), window(1, 1, q)
        psi[q, 0] = trans_real * back_real + trans_imag * back_imag
        psi[q, 1] = trans_real * back_imag - trans_imag * back_real
        return carry

    for q in range(slots):
        second_layer(q, 0)
    strip = range(lane_tiles, all_tiles)
    own = range(lane_tiles)

    gather(1, strip, tile, patch)
    start_corners(1)
    gather(1, strip, 0, tile)
    put_bottom(1).start()
    probe_part[...] = jnp.zeros(probe_part.shape, F32)

    def third_layer(q, carry):
        freq_real, freq_imag = forward(psi[q, 0], psi[q, 1], tables)
        back_real, back_imag = backward(
            prop[0] * freq_real + prop[1] * freq_imag,
            prop[0] * freq_imag - prop[1] * freq_real,
            tables,
        )
        deposit(0, q, 0, probe[0] * back_real + probe[1] * back_imag)
        deposit(0, q, 1, probe[0] * back_imag - probe[1] * back_real)
        weight = live[q].astype(F32)
        probe_part[0] += weight * (trans[q, 0] * back_real + trans[q, 1] * back_imag)
        probe_part[1] += weight * (trans[q, 0] * back_imag - trans[q, 1] * back_real)
        return carry

    for q in range(slots):
        third_layer(q, 0)
    pair_sum().start()
    for j in range(strip_tiles):
        add_corner(1, j)
    after_pair()
    put_top(1, 0).start()
    gather(0, strip, tile, patch)
    start_corners(0)
    gather(1, own, tile, patch)
    put_below(1).start()
    gather(0, strip, 0, tile)
    gather(0, own, tile, patch)
    gather(1, own, 0, tile)
    after_row()
    put_top(1, 1).start()
    gather(0, own, 0, tile)
    after_outer()
    put_bottom(0).start()
    add_corner(0, 0)
    after_inner()
    put_top(0, 0).start()
    add_corner(0, 1)
    after_outer_gather()
    put_top(0, 1).start()
    put_below(0).start()
    finish_put(1)
    after_row_gather()
    finish_put(0)
    finish_sum()
    for s in range(layers):
        put_bottom(s).wait_send()
        put_below(s).wait_send()
        for j in range(strip_tiles):
            put_corner(s, j).wait_send()
            put_top(s, j).wait_send()


def step_call(n_ty, n_tx, scaling, *operands):
    obj, probe, phase, amplitude, _, _, tables, chosen = operands
    layers, _, tile, _ = obj.shape
    patch = probe.shape[1]
    slots = amplitude.shape[0]
    lane_tiles, strip_tiles = tile // LANES, patch // LANES
    all_tiles = lane_tiles + strip_tiles
    gets = 3 * strip_tiles + lane_tiles
    puts = 2 * strip_tiles + 2
    n_row, n_outer = n_ty // 2, n_tx // INNER
    row_rows = patch // n_row
    chunk = row_rows // n_outer
    sums = 2 * n_row + 2 * n_outer + INNER + 2
    vmem = pl.BlockSpec(memory_space=pltpu.VMEM)
    smem = pl.BlockSpec(memory_space=pltpu.SMEM)
    whole = pl.BlockSpec(memory_space=pl.ANY)
    return pl.pallas_call(
        functools.partial(step_kernel, n_ty, n_tx, scaling),
        name="step",
        out_shape=(
            pltpu.VMEM(obj.shape, F32),
            pltpu.VMEM((2, n_row, n_outer, chunk, patch), F32),
        ),
        in_specs=[whole, whole, whole, whole, smem, smem, whole, whole],
        out_specs=(vmem, vmem),
        scratch_shapes=[
            pltpu.VMEM((2, all_tiles, tile + patch, LANES), F32),
            pltpu.VMEM((2, all_tiles, tile + patch, LANES), F32),
            pltpu.VMEM((slots, 2, strip_tiles + 1, 2 * tile + patch, LANES), F32),
            pltpu.VMEM((slots, 2, strip_tiles + 1, 2 * tile + patch, LANES), F32),
            pltpu.VMEM((layers, 2, all_tiles, tile + patch, LANES), F32),
            pltpu.VMEM((layers, 2, strip_tiles, tile, LANES), F32),
            pltpu.VMEM((layers, 2, all_tiles, patch, LANES), F32),
            pltpu.VMEM((slots, 2, patch, patch), F32),
            pltpu.VMEM((slots, 2, patch, patch), F32),
            pltpu.VMEM((2, patch, patch), F32),
            pltpu.VMEM((slots, patch, patch), F32),
            pltpu.VMEM((2, patch, patch), F32),
            pltpu.VMEM((patch, patch), F32),
            pltpu.VMEM((n_row, row_rows, patch), F32),
            pltpu.VMEM((n_row, row_rows, patch), F32),
            pltpu.VMEM((n_outer, chunk, patch), F32),
            pltpu.VMEM((n_outer, chunk, patch), F32),
            pltpu.VMEM((INNER, chunk, patch), F32),
            pltpu.VMEM(probe.shape, F32),
            pltpu.VMEM(phase.shape, F32),
            pltpu.VMEM(amplitude.shape, F32),
            pltpu.VMEM(tables.shape, BF16),
            pltpu.VMEM(chosen.shape, BF16),
            pltpu.SemaphoreType.DMA((layers, lane_tiles)),
            pltpu.SemaphoreType.DMA((5,)),
            pltpu.SemaphoreType.DMA((layers, gets)),
            pltpu.SemaphoreType.DMA((layers, gets)),
            pltpu.SemaphoreType.DMA((layers, puts)),
            pltpu.SemaphoreType.DMA((layers, puts)),
            pltpu.SemaphoreType.DMA((sums,)),
            pltpu.SemaphoreType.DMA((sums,)),
        ],
        compiler_params=pltpu.CompilerParams(
            collective_id=0, has_side_effects=True, vmem_limit_bytes=57 * 1024 * 1024
        ),
    )(*operands)


def copy_kernel(grad, shared, grad_out, shared_out, sem):
    copies = [
        pltpu.make_async_copy(grad.at[s, part], grad_out.at[s, part], sem.at[2 * s + part])
        for s in range(grad.shape[0])
        for part in range(2)
    ]
    copies.append(pltpu.make_async_copy(shared, shared_out, sem.at[len(copies)]))
    for copy in copies:
        copy.start()
    for copy in copies:
        copy.wait()


def copy_call(grad, shared):
    whole = pl.BlockSpec(memory_space=pl.ANY)
    vmem = pl.BlockSpec(memory_space=pltpu.VMEM)
    return pl.pallas_call(
        copy_kernel,
        name="hand_over",
        out_shape=(
            jax.ShapeDtypeStruct(grad.shape, F32),
            jax.ShapeDtypeStruct(shared.shape, F32),
        ),
        in_specs=[vmem, vmem],
        out_specs=(whole, whole),
        scratch_shapes=[pltpu.SemaphoreType.DMA((2 * grad.shape[0] + 1,))],
    )(grad, shared)


def solution(mesh):
    n_ty, n_tx = mesh.shape["ty"], mesh.shape["tx"]

    def per_device(object_field, probe_wave, prop_phase, amplitude, offsets, live_slots):
        patch = probe_wave.shape[1]
        scaling = 1.0 / math.sqrt(live_slots.shape[0] * n_ty * n_tx)
        owned, shared = step_call(
            n_ty,
            n_tx,
            scaling,
            object_field,
            probe_wave,
            prop_phase,
            amplitude,
            offsets,
            live_slots,
            jnp.asarray(dft_halves(patch)),
            jnp.asarray(even_odd(patch)),
        )
        owned = pltpu.with_memory_space_constraint(owned, pltpu.VMEM)
        shared = pltpu.with_memory_space_constraint(shared, pltpu.VMEM)
        owned, shared = copy_call(owned, shared)
        return owned, shared.reshape(probe_wave.shape)

    placed = (
        P(None, None, "ty", "tx"),
        P(),
        P(),
        P(("ty", "tx"), None, None),
        P(None, ("ty", "tx")),
        P(("ty", "tx")),
    )
    return jax.shard_map(
        per_device,
        mesh=mesh,
        in_specs=placed,
        out_specs=(P(None, None, "ty", "tx"), P()),
        check_vma=False,
    )
```
